512 devices in a mesh: row: 16 (over z, core), col: 32 (over y, x).
Axes of the slice: x: 4, y: 8, z: 8, core: 2. Of those that a mesh axis runs over, the one named last changes fastest.
Arguments:
- source: bfloat16 [8192, 1024], P(('row', 'col')), may hold values from -6 to 6
- target: bfloat16 [65536, 1024], P(('col', 'row')), may hold values from -16 to 16
- source_mass: float32 [8192], P('row'), may hold values from 0.5 to 2
- target_mass: float32 [65536], P('col'), may hold values from 0.5 to 2
- tile_src: int32 [16, 32, 32], P('row', 'col'), may hold values from 0 to 3, as said below
- tile_dst: int32 [16, 32, 32], P('row', 'col'), may hold values from 0 to 15, as said below
- tile_count: int32 [16, 32], P('row', 'col'), may hold values from 16 to 32, as said below
Outputs:
- source_potential: float32 [8192], P('row')
- target_potential: float32 [65536], P('col')
- mapped: bfloat16 [8192, 1024], P(('row', 'col'))
The draws below stay inside these ranges and needn't reach their ends.
Inputs may be any that keep to these rules, and one draw needn't show every extreme that they name: Within one grid cell the listed (tile_src, tile_dst) pairs are all different; entries at k >= tile_count are valid cluster numbers but not part of the support. Every source cluster of every grid row and every target cluster of every grid column is live in some grid cell. `tile_dst`: see tile_src. `tile_count`: some grid cell has exactly 32 live tiles in every draw; counts are uneven over cells.
All inputs are finite; a program needn't handle non-finite values.
Results may differ from the reference program's by a relative error of at most 0.0055.
Values may be sent and summed in bfloat16 or wider, within the bound.
No kernel may reach another device: no remote copies, remote signals or barrier semaphores. Data moves between devices by JAX's collectives and lax.ppermute only.
A program may use at most 64 MiB of HBM per device.

```python
import math
import jax
import jax.numpy as jnp
from jax import lax

D = 1024
BLK = 128
ITERS = 3
ROWB = 16
COLB = 32
SRC_ROWS_BLK = 512
TGT_ROWS_BLK = 2048
SBLOCKS = 4
TBLOCKS = 16
TILES = 32
NS = 8192
NT = 65536


def tile_table(key):
    cells = ROWB * COLB
    pairs = SBLOCKS * TBLOCKS
    keys = jax.random.split(jax.random.fold_in(key, 7), cells)
    perms = jax.vmap(lambda sub: jax.random.permutation(sub, pairs))(keys)
    inverse = jnp.argsort(perms, axis=1).astype(jnp.int32)
    cell = jnp.arange(cells, dtype=jnp.int32)
    rowi = cell // COLB
    coli = cell % COLB
    forced = coli % SBLOCKS * TBLOCKS + rowi % TBLOCKS
    rank = jnp.where(jnp.arange(pairs, dtype=jnp.int32)[None, :] == forced[:, None], -1, inverse)
    order = jnp.argsort(rank, axis=1)[:, :TILES].astype(jnp.int32)
    counts = jax.random.randint(jax.random.fold_in(key, 11), (cells,), max(TILES // 2, 1), TILES + 1)
    chosen = jax.random.randint(jax.random.fold_in(key, 13), (), 0, cells)
    counts = jnp.where(cell == chosen, TILES, counts).astype(jnp.int32)
    src = (order // TBLOCKS).reshape(ROWB, COLB, TILES)
    dst = (order % TBLOCKS).reshape(ROWB, COLB, TILES)
    return (src, dst, counts.reshape(ROWB, COLB))


def draw_tile_src(key, part):
    return tile_table(key)[0]


def draw_tile_dst(key, part):
    return tile_table(key)[1]


def draw_tile_count(key, part):
    return tile_table(key)[2]


def steps_of(key, dims, cuts, least, top_value):
    loudness, own = 1.0, jax.random.fold_in(key, 6)
    for axis_at, parts in cuts:
        heights = jnp.exp(jax.random.uniform(jax.random.fold_in(own, axis_at), (parts,), jnp.float32, least / len(cuts), top_value / len(cuts)))
        loudness = loudness * jnp.repeat(heights, dims[axis_at] // parts).reshape([-1 if axis == axis_at else 1 for axis in range(len(dims))])
    return loudness


def scatter_about(rng, shape, deviation, limit, cuts=(), kind=jnp.bfloat16):
    level = steps_of(rng, shape, cuts, -0.22, 0.18) if cuts else 1.0
    array = jax.random.normal(rng, shape, jnp.float32) * deviation * level
    return jnp.minimum(jnp.maximum(array, -limit), limit).astype(kind)


def setup_inputs(seed: int = 0) -> dict:
    key_list = jax.random.split(jax.random.key(seed), 8)
    source = scatter_about(key_list[0], (NS, D), 1.0, 6.0, ((0, 512),))
    target = scatter_about(key_list[1], (NT, D), 2.5, 16.0, ((0, 512),))
    source_mass = jnp.clip(jnp.exp(math.log(2.0) - 1.3862944 * jax.random.uniform(key_list[2], (NS,), jnp.float32) ** steps_of(key_list[2], (NS,), ((0, 16),), -0.2, 0.2)), 0.5, 2.0)
    target_mass = jnp.clip(jnp.exp(math.log(2.0) - 1.3862944 * jax.random.uniform(key_list[3], (NT,), jnp.float32) ** steps_of(key_list[3], (NT,), ((0, 32),), -0.2, 0.2)), 0.5, 2.0)
    tile_src = draw_tile_src(jax.random.fold_in(key_list[7], 71), 0)
    tile_dst = draw_tile_dst(jax.random.fold_in(key_list[7], 71), 0)
    tile_count = draw_tile_count(jax.random.fold_in(key_list[7], 71), 0)
    return {"source": source, "target": target, "source_mass": source_mass, "target_mass": target_mass, "tile_src": tile_src, "tile_dst": tile_dst, "tile_count": tile_count}


EPS = 0.02
FLOOR = -1.0e30


def partial_lse(logits, own_idx, valid, nblocks):
    tile_max = jnp.where(valid[:, None], jnp.max(logits, axis=2), FLOOR)
    member = (own_idx[:, None] == jnp.arange(nblocks, dtype=jnp.int32)[None, :]) & valid[:, None]
    blk_max = jnp.max(jnp.where(member[:, :, None], tile_max[:, None, :], FLOOR), axis=0)
    shift = jnp.take(blk_max, own_idx, axis=0)
    tile_sum = jnp.where(valid[:, None], jnp.sum(jnp.exp(logits - shift[:, :, None]), axis=2), 0.0)
    blk_sum = jnp.einsum("kn,ki->ni", member.astype(jnp.float32), tile_sum, precision=lax.Precision.HIGHEST)
    return blk_max.reshape(-1), blk_sum.reshape(-1)


def reference(source, target, source_mass, target_mass, tile_src, tile_dst, tile_count):
    src_blocks = source.reshape(ROWB, SRC_ROWS_BLK, D)
    tgt_blocks = target.reshape(COLB, TGT_ROWS_BLK, D)
    src_norms = jnp.sum(jnp.square(src_blocks.astype(jnp.float32)), axis=2)
    tgt_norms = jnp.sum(jnp.square(tgt_blocks.astype(jnp.float32)), axis=2)
    log_a = jnp.log(source_mass).reshape(ROWB, SRC_ROWS_BLK)
    log_b = jnp.log(target_mass).reshape(COLB, TGT_ROWS_BLK)
    cells = jnp.arange(ROWB * COLB, dtype=jnp.int32)

    def costs_of(cell):
        rowi = cell // COLB
        coli = cell % COLB
        sidx = tile_src[rowi, coli].astype(jnp.int32)
        tidx = tile_dst[rowi, coli].astype(jnp.int32)
        valid = jnp.arange(TILES, dtype=jnp.int32) < tile_count[rowi, coli]
        xs = src_blocks[rowi].reshape(SBLOCKS, BLK, D)[sidx].astype(jnp.float32)
        ys = tgt_blocks[coli].reshape(TBLOCKS, BLK, D)[tidx].astype(jnp.float32)
        cross = jnp.einsum("kid,kjd->kij", xs, ys, precision=lax.Precision.HIGHEST)
        norm_s = src_norms[rowi].reshape(SBLOCKS, BLK)[sidx]
        norm_t = tgt_norms[coli].reshape(TBLOCKS, BLK)[tidx]
        costs = (norm_s[:, :, None] + norm_t[:, None, :] - 2.0 * cross) / D
        return rowi, coli, sidx, tidx, valid, costs, ys

    potential_g = jnp.zeros((COLB, TGT_ROWS_BLK), jnp.float32)
    potential_f = jnp.zeros((ROWB, SRC_ROWS_BLK), jnp.float32)
    for step in range(ITERS):
        def f_part(cell):
            rowi, coli, sidx, tidx, valid, costs, ys = costs_of(cell)
            g_tiles = potential_g[coli].reshape(TBLOCKS, BLK)[tidx]
            return partial_lse((g_tiles[:, None, :] - costs) / EPS, sidx, valid, SBLOCKS)

        peaks, sums = lax.map(f_part, cells)
        peaks = peaks.reshape(ROWB, COLB, SRC_ROWS_BLK)
        sums = sums.reshape(ROWB, COLB, SRC_ROWS_BLK)
        big = jnp.max(peaks, axis=1)
        total = jnp.sum(sums * jnp.exp(peaks - big[:, None, :]), axis=1)
        potential_f = EPS * log_a - EPS * (big + jnp.log(total))

        def g_part(cell):
            rowi, coli, sidx, tidx, valid, costs, ys = costs_of(cell)
            f_tiles = potential_f[rowi].reshape(SBLOCKS, BLK)[sidx]
            logits = jnp.swapaxes((f_tiles[:, :, None] - costs) / EPS, 1, 2)
            return partial_lse(logits, tidx, valid, TBLOCKS)

        peaks, sums = lax.map(g_part, cells)
        peaks = peaks.reshape(ROWB, COLB, TGT_ROWS_BLK)
        sums = sums.reshape(ROWB, COLB, TGT_ROWS_BLK)
        big = jnp.max(peaks, axis=0)
        total = jnp.sum(sums * jnp.exp(peaks - big[None, :, :]), axis=0)
        potential_g = EPS * log_b - EPS * (big + jnp.log(total))

    def add_cell(cell, carry):
        numer, denom = carry
        rowi, coli, sidx, tidx, valid, costs, ys = costs_of(cell)
        f_tiles = potential_f[rowi].reshape(SBLOCKS, BLK)[sidx]
        g_tiles = potential_g[coli].reshape(TBLOCKS, BLK)[tidx]
        weights = jnp.where(valid[:, None, None], jnp.exp((f_tiles[:, :, None] + g_tiles[:, None, :] - costs) / EPS), 0.0)
        member = (sidx[:, None] == jnp.arange(SBLOCKS, dtype=jnp.int32)[None, :]).astype(jnp.float32)
        low = weights.astype(jnp.bfloat16).astype(jnp.float32)
        mass = jnp.einsum("kn,ki->ni", member, jnp.sum(low, axis=2), precision=lax.Precision.HIGHEST)
        tile_num = jnp.einsum("kij,kjd->kid", low, ys, precision=lax.Precision.HIGHEST)
        cell_num = jnp.einsum("kn,kid->nid", member, tile_num, precision=lax.Precision.HIGHEST)
        numer = numer.at[rowi].add(cell_num.reshape(SRC_ROWS_BLK, D))
        denom = denom.at[rowi].add(mass.reshape(SRC_ROWS_BLK))
        return numer, denom

    numer0 = jnp.zeros((ROWB, SRC_ROWS_BLK, D), jnp.float32)
    denom0 = jnp.zeros((ROWB, SRC_ROWS_BLK), jnp.float32)
    numer, denom = lax.fori_loop(0, ROWB * COLB, add_cell, (numer0, denom0))
    mapped = (numer / denom[:, :, None]).astype(jnp.bfloat16).reshape(NS, D)
    return potential_f.reshape(NS), potential_g.reshape(NT), mapped
```

```python
import math

import jax
import jax.numpy as jnp
from jax import lax
from jax.experimental import pallas as pl
from jax.experimental.pallas import tpu as pltpu
from jax.sharding import PartitionSpec as P

BLK = 128
ITERS = 3
EPS = 0.02
UNIT = EPS * math.log(2.0)
FAR = 1e30
MIB = 1 << 20


def nt_dot(a, b):
    return lax.dot_general(a, b, (((1,), (1,)), ((), ())), preferred_element_type=jnp.float32)


def lanes_of(row):
    return jnp.transpose(jnp.broadcast_to(row, (BLK, BLK)))


def finish_rows(peak, total):
    peak, total = jnp.transpose(peak), jnp.transpose(total)
    top = jnp.max(peak, axis=0, keepdims=True)
    return top + jnp.log2(jnp.sum(total * jnp.exp2(peak - top), axis=0, keepdims=True))


def put_copies(out_ref, row_at, row):
    copies = out_ref.shape[0]
    for k in range(copies):
        out_ref[k, pl.ds(row_at, 1), :] = row


def cost_kernel(sidx, tidx, live, src_ref, tgt_ref, cost_ref, part_ref, far, snorm, peak, total):
    step = pl.program_id(0)
    nsrc = src_ref.shape[0] // BLK
    per = tgt_ref.shape[0] // BLK
    width = src_ref.shape[1]
    scale = 1.0 / (width * UNIT)

    @pl.when(step == 0)
    def _():
        for i in range(far.shape[0]):
            far[i] = FAR

        def mark(k, c):
            far[sidx[k] * (far.shape[0] // nsrc) + tidx[k]] = 0.0
            return c

        lax.fori_loop(0, live[0], mark, 0)
        for s in range(nsrc):
            rows = src_ref[s * BLK : (s + 1) * BLK, :].astype(jnp.float32)
            norm = jnp.sum(rows * rows, axis=1, keepdims=True) * scale
            snorm[s * BLK : (s + 1) * BLK, :] = jnp.broadcast_to(norm, (BLK, BLK))
        peak[...] = jnp.full_like(peak, -FAR)
        total[...] = jnp.zeros_like(total)

    rows = tgt_ref[...].astype(jnp.float32)
    square = rows * rows
    high = square.astype(jnp.bfloat16)
    low = (square - high.astype(jnp.float32)).astype(jnp.bfloat16)
    ones = jnp.ones((8, width), jnp.bfloat16)
    tnorm = (nt_dot(ones, high) + nt_dot(ones, low))[0:1, :] * scale
    nall = far.shape[0] // nsrc
    for s in range(nsrc):
        at = slice(s * BLK, (s + 1) * BLK)
        cross = nt_dot(src_ref[at, :], tgt_ref[...]) * (-2.0 * scale)
        tiles = []
        for t in range(per):
            lanes = slice(t * BLK, (t + 1) * BLK)
            away = tnorm[:, lanes] + far[s * nall + step * per + t]
            tile = cross[:, lanes] + snorm[at, :] + away
            cost_ref[at, lanes] = tile
            tiles.append(tile)
        old = peak[at, :]
        new = old
        for tile in tiles:
            new = jnp.maximum(new, -tile)
        acc = total[at, :] * jnp.exp2(old - new)
        for tile in tiles:
            acc = acc + jnp.exp2(-tile - new)
        peak[at, :] = new
        total[at, :] = acc

    @pl.when(step == pl.num_programs(0) - 1)
    def _():
        for s in range(nsrc):
            at = slice(s * BLK, (s + 1) * BLK)
            put_copies(part_ref, s, finish_rows(peak[at, :], total[at, :]))


def combine(log_mass, parts_ref):
    parts = parts_ref[...]
    top = jnp.max(parts, axis=0)
    return log_mass - (top + jnp.log2(jnp.sum(jnp.exp2(parts - top[None]), axis=0)))


def target_kernel(parts_ref, mass_ref, cost_ref, pot_ref, part_ref, wide):
    pot = combine(jnp.log2(mass_ref[...]), parts_ref)
    pot_ref[...] = pot
    nsrc, ntgt = pot.shape[0], cost_ref.shape[1] // BLK
    for s in range(nsrc):
        wide[s * BLK : (s + 1) * BLK, :] = lanes_of(pot[s : s + 1, :])
    for t in range(ntgt):
        lanes = slice(t * BLK, (t + 1) * BLK)
        gap = (wide[...] - cost_ref[:, lanes]).reshape(-1, 8, BLK)
        peak = jnp.max(gap, axis=0)
        top = jnp.max(peak, axis=0, keepdims=True)
        total = jnp.sum(jnp.exp2(gap - top[None]), axis=0)
        row = top + jnp.log2(jnp.sum(total, axis=0, keepdims=True))
        put_copies(part_ref, t, row)


def source_kernel(parts_ref, mass_ref, cost_ref, part_ref):
    pot = combine(jnp.log2(mass_ref[...]), parts_ref)
    ntgt, nsrc = pot.shape[0], cost_ref.shape[0] // BLK
    for s in range(nsrc):
        at = slice(s * BLK, (s + 1) * BLK)

        def gap(t):
            return pot[t : t + 1, :] - cost_ref[at, t * BLK : (t + 1) * BLK]

        peak = gap(0)
        for t in range(1, ntgt):
            peak = jnp.maximum(peak, gap(t))
        total = jnp.exp2(gap(0) - peak)
        for t in range(1, ntgt):
            total = total + jnp.exp2(gap(t) - peak)
        put_copies(part_ref, s, finish_rows(peak, total))


def map_kernel(parts_ref, mass_ref, fpot_ref, cost_ref, tgt_ref, pot_ref, sums_ref, weight):
    pot = combine(jnp.log2(mass_ref[...]), parts_ref)
    pot_ref[...] = pot
    ntgt, nsrc = pot.shape[0], cost_ref.shape[0] // BLK
    width = tgt_ref.shape[1]
    for s in range(nsrc):
        at = slice(s * BLK, (s + 1) * BLK)
        mine = lanes_of(fpot_ref[s : s + 1, :])
        for t in range(ntgt):
            lanes = slice(t * BLK, (t + 1) * BLK)
            power = jnp.exp2(mine + pot[t : t + 1, :] - cost_ref[at, lanes])
            weight[at, lanes] = power.astype(jnp.bfloat16)
    low = weight[...]
    for d in range(0, width, 256):
        part = jnp.dot(low, tgt_ref[:, d : d + 256], preferred_element_type=jnp.float32)
        sums_ref[:, d : d + 256] = part.astype(jnp.bfloat16)
    total = jnp.dot(low, jnp.ones((low.shape[1], BLK), jnp.bfloat16), preferred_element_type=jnp.float32)
    high = total.astype(jnp.bfloat16).astype(jnp.float32)
    lane = lax.broadcasted_iota(jnp.int32, total.shape, 1)
    sums_ref[:, width:] = jnp.where(lane == 0, high, total - high).astype(jnp.bfloat16)


def divide_kernel(sums_ref, out_ref):
    width = out_ref.shape[1]
    sums = sums_ref[0].astype(jnp.float32)
    for k in range(1, sums_ref.shape[0]):
        sums = sums + sums_ref[k].astype(jnp.float32)
    total = sums[:, width : width + 1] + sums[:, width + 1 : width + 2]
    out_ref[...] = (sums[:, :width] / total).astype(out_ref.dtype)


def whole(n):
    return [pl.BlockSpec(memory_space=pltpu.VMEM)] * n


def call(kernel, shapes, scratch, args, limit, flops=0):
    return pl.pallas_call(
        kernel,
        out_shape=shapes,
        in_specs=whole(len(args)),
        out_specs=jax.tree.map(lambda _: pl.BlockSpec(memory_space=pltpu.VMEM), shapes),
        scratch_shapes=scratch,
        compiler_params=pltpu.CompilerParams(vmem_limit_bytes=limit * MIB),
    )(*args)


def shape(*dims, dtype=jnp.float32):
    return jax.ShapeDtypeStruct(dims, dtype)


def spread(x, axis):
    return lax.all_to_all(x, axis, 0, 0, tiled=True)


def body(source, target, source_mass, target_mass, tile_src, tile_dst, tile_count):
    rows, cols = lax.axis_size("row"), lax.axis_size("col")
    width = source.shape[1]
    tgt = lax.all_gather(target, "row", axis=0, tiled=True)
    src = spread(jnp.broadcast_to(source[None], (cols, *source.shape)), "col")
    src = src.reshape(-1, width)
    nsrc, ntgt = src.shape[0] // BLK, tgt.shape[0] // BLK
    amass = source_mass.reshape(nsrc, BLK)
    bmass = target_mass.reshape(ntgt, BLK)

    per = 2
    cost, part = pl.pallas_call(
        cost_kernel,
        out_shape=(shape(src.shape[0], tgt.shape[0]), shape(cols, nsrc, BLK)),
        grid_spec=pltpu.PrefetchScalarGridSpec(
            num_scalar_prefetch=3,
            grid=(ntgt // per,),
            in_specs=[
                pl.BlockSpec(src.shape, lambda t, *_: (0, 0)),
                pl.BlockSpec((per * BLK, width), lambda t, *_: (t, 0)),
            ],
            out_specs=(
                pl.BlockSpec((src.shape[0], per * BLK), lambda t, *_: (0, t)),
                pl.BlockSpec((cols, nsrc, BLK), lambda t, *_: (0, 0, 0)),
            ),
            scratch_shapes=[
                pltpu.SMEM((nsrc * ntgt,), jnp.float32),
                pltpu.VMEM((src.shape[0], BLK), jnp.float32),
                pltpu.VMEM((src.shape[0], BLK), jnp.float32),
                pltpu.VMEM((src.shape[0], BLK), jnp.float32),
            ],
        ),
        compiler_params=pltpu.CompilerParams(vmem_limit_bytes=24 * MIB),
    )(tile_src.reshape(-1), tile_dst.reshape(-1), tile_count.reshape(-1), src, tgt)

    for step in range(ITERS):
        fpot, part = call(
            target_kernel,
            (shape(nsrc, BLK), shape(rows, ntgt, BLK)),
            [pltpu.VMEM((src.shape[0], BLK), jnp.float32)],
            (spread(part, "col"), amass, cost),
            16,
        )
        parts = spread(part, "row")
        if step < ITERS - 1:
            part = call(source_kernel, shape(cols, nsrc, BLK), [], (parts, bmass, cost), 16)
    gpot, sums = call(
        map_kernel,
        (shape(ntgt, BLK), shape(src.shape[0], width + BLK, dtype=jnp.bfloat16)),
        [pltpu.VMEM(cost.shape, jnp.bfloat16)],
        (parts, bmass, fpot, cost, tgt),
        32,
    )
    share = src.shape[0] // cols
    sums = spread(sums.reshape(cols, share, width + BLK), "col")
    mapped = call(divide_kernel, shape(share, width, dtype=jnp.bfloat16), [], (sums,), 8)
    return (fpot.reshape(-1) * UNIT, gpot.reshape(-1) * UNIT, mapped)


def solution(mesh):
    in_specs = (
        P(("row", "col"), None),
        P(("col", "row"), None),
        P("row"),
        P("col"),
        P("row", "col", None),
        P("row", "col", None),
        P("row", "col"),
    )
    out_specs = (P("row"), P("col"), P(("row", "col"), None))
    return jax.shard_map(body, mesh=mesh, in_specs=in_specs, out_specs=out_specs, check_vma=False)
```

```python
import math

import jax
import jax.numpy as jnp
import numpy as np
from jax import lax
from jax.experimental import pallas as pl
from jax.experimental.pallas import tpu as pltpu
from jax.sharding import PartitionSpec as P

BLK = 128
ITERS = 3
EPS = 0.02
UNIT = EPS * math.log(2.0)
FAR = 1e30
MIB = 1 << 20
CHIPS, CORES = 8, 2
COLY, COLX = 8, 4
CHUNK = 256


def nt_dot(a, b):
    return lax.dot_general(a, b, (((1,), (1,)), ((), ())), preferred_element_type=jnp.float32)


def square_sums(rows):
    rows = rows.astype(jnp.float32)
    rows = rows * rows
    total = rows[:, :BLK]
    for d in range(BLK, rows.shape[1], BLK):
        total = total + rows[:, d : d + BLK]
    return total


def lanes_of(row):
    return jnp.transpose(jnp.broadcast_to(row, (BLK, BLK)))


def finish_rows(peak, total):
    peak, total = jnp.transpose(peak), jnp.transpose(total)
    top = jnp.max(peak, axis=0, keepdims=True)
    return top + jnp.log2(jnp.sum(total * jnp.exp2(peak - top), axis=0, keepdims=True))


def tiles_of(cost_refs):
    return [(ref, slice(d, d + BLK)) for ref in cost_refs for d in range(0, ref.shape[1], BLK)]


def source_parts(cost_refs, pot_row, part_ref):
    tiles = tiles_of(cost_refs)
    for s in range(cost_refs[0].shape[0] // BLK):
        at = slice(s * BLK, (s + 1) * BLK)

        def gap(n):
            ref, lanes = tiles[n]
            return pot_row(n) - ref[at, lanes]

        peak = gap(0)
        for n in range(1, len(tiles)):
            peak = jnp.maximum(peak, gap(n))
        total = jnp.exp2(gap(0) - peak)
        for n in range(1, len(tiles)):
            total = total + jnp.exp2(gap(n) - peak)
        row = finish_rows(peak, total)
        for k in range(part_ref.shape[0]):
            part_ref[k, s : s + 1, :] = row


def cost_kernel(first, npiece, last, *refs):
    order, sidx, tidx, live, src_ref, *refs = refs
    pieces, refs = refs[:npiece], refs[npiece:]
    if first == 0:
        cost_ref, norm_ref, far = refs
    elif last:
        norm_ref, *held, cost_ref, part_ref, far = refs
    else:
        norm_ref, cost_ref, far = refs
    nsrc = src_ref.shape[0] // BLK
    ntgt = far.shape[0] // nsrc
    scale = 1.0 / (src_ref.shape[1] * UNIT)
    for i in range(far.shape[0]):
        far[i] = FAR

    def mark(k, c):
        far[sidx[k] * ntgt + tidx[k]] = 0.0
        return c

    lax.fori_loop(0, live[0], mark, 0)
    if first == 0:
        for s in range(nsrc):
            at = slice(s * BLK, (s + 1) * BLK)
            norm = jnp.sum(square_sums(src_ref[at, :]), axis=1, keepdims=True) * scale
            norm_ref[at, :] = jnp.broadcast_to(norm, (BLK, BLK))
    slot, lane = first, 0
    for piece in pieces:
        count = piece.shape[0] // BLK
        away = []
        for t in range(count):
            sums = jnp.transpose(square_sums(piece[t * BLK : (t + 1) * BLK, :]))
            away.append(jnp.sum(sums, axis=0, keepdims=True) * scale)
        for s in range(nsrc):
            at = slice(s * BLK, (s + 1) * BLK)
            cross = nt_dot(src_ref[at, :], piece[...]) * (-2.0 * scale)
            for t in range(count):
                far_off = far[s * ntgt + order[slot + t]]
                tile = cross[:, t * BLK : (t + 1) * BLK] + norm_ref[at, :] + (away[t] + far_off)
                cost_ref[at, lane + t * BLK : lane + (t + 1) * BLK] = tile
        slot += count
        lane += count * BLK
    if last:
        source_parts([*held, cost_ref], lambda n: 0.0, part_ref)


def combine(mass_ref, parts_ref):
    parts = parts_ref[...]
    top = jnp.max(parts, axis=0)
    low = jnp.log2(jnp.sum(jnp.exp2(parts - top[None]), axis=0))
    return jnp.log2(mass_ref[...]) - (top + low)


def target_kernel(order, parts_ref, mass_ref, *refs):
    *cost_refs, pot_ref, part_ref, wide, mine = refs
    pot = combine(mass_ref, parts_ref)
    pot_ref[...] = pot
    for s in range(pot.shape[0]):
        wide[s * BLK : (s + 1) * BLK, :] = lanes_of(pot[s : s + 1, :])
    for n, (ref, lanes) in enumerate(tiles_of(cost_refs)):
        gap = (wide[...] - ref[:, lanes]).reshape(-1, 8, BLK)
        peak = jnp.max(gap, axis=0)
        top = jnp.max(peak, axis=0, keepdims=True)
        total = jnp.sum(jnp.exp2(gap - top[None]), axis=0)
        mine[pl.ds(order[n], 1), :] = top + jnp.log2(jnp.sum(total, axis=0, keepdims=True))
    part_ref[...] = jnp.broadcast_to(mine[...][None], part_ref.shape)


def source_kernel(order, parts_ref, mass_ref, *refs):
    *cost_refs, part_ref, pot_ref = refs
    pot_ref[...] = combine(mass_ref, parts_ref)
    rows = [pot_ref[pl.ds(order[n], 1), :] for n in range(pot_ref.shape[0])]
    source_parts(cost_refs, lambda n: rows[n], part_ref)


def map_kernel(npiece, order, parts_ref, mass_ref, fpot_ref, *refs):
    pieces, refs = refs[:npiece], refs[npiece:]
    *cost_refs, pot_ref, sums_ref, weight = refs
    pot_ref[...] = combine(mass_ref, parts_ref)
    nsrc = cost_refs[0].shape[0] // BLK
    width = pieces[0].shape[1]
    for s in range(nsrc):
        at = slice(s * BLK, (s + 1) * BLK)
        mine = lanes_of(fpot_ref[s : s + 1, :])
        for n, (ref, lanes) in enumerate(tiles_of(cost_refs)):
            power = jnp.exp2(mine + pot_ref[pl.ds(order[n], 1), :] - ref[at, lanes])
            weight[at, n * BLK : (n + 1) * BLK] = power.astype(jnp.bfloat16)

    share = sums_ref.shape[1] // COLY

    def put(block, lanes):
        for y in range(COLY):
            for x in range(COLX):
                k = (y * COLX + x) * share
                sums_ref[x, y * share : (y + 1) * share, lanes] = block[k : k + share, :]

    for d in range(0, width, CHUNK):
        part, lane = None, 0
        for piece in pieces:
            low = weight[:, lane : lane + piece.shape[0]]
            add = jnp.dot(low, piece[:, d : d + CHUNK], preferred_element_type=jnp.float32)
            part = add if part is None else part + add
            lane += piece.shape[0]
        put(part.astype(jnp.bfloat16), slice(d, d + CHUNK))
    ones = jnp.ones((weight.shape[1], BLK), jnp.bfloat16)
    total = jnp.dot(weight[...], ones, preferred_element_type=jnp.float32)
    put(two_pieces(total), slice(width, width + BLK))


def two_pieces(total):
    high = total.astype(jnp.bfloat16).astype(jnp.float32)
    lane = lax.broadcasted_iota(jnp.int32, total.shape, 1)
    return jnp.where(lane == 0, high, total - high).astype(jnp.bfloat16)


def add_up(sums_ref):
    sums = sums_ref[0].astype(jnp.float32)
    for k in range(1, sums_ref.shape[0]):
        sums = sums + sums_ref[k].astype(jnp.float32)
    return sums


def add_kernel(sums_ref, out_ref):
    width = out_ref.shape[1] - BLK
    sums = add_up(sums_ref)
    total = sums[:, width : width + 1] + sums[:, width + 1 : width + 2]
    out_ref[:, :width] = sums[:, :width].astype(jnp.bfloat16)
    out_ref[:, width:] = two_pieces(jnp.broadcast_to(total, (total.shape[0], BLK)))


def divide_kernel(sums_ref, out_ref):
    width = out_ref.shape[1]
    sums = add_up(sums_ref)
    total = sums[:, width : width + 1] + sums[:, width + 1 : width + 2]
    out_ref[...] = (sums[:, :width] / total).astype(out_ref.dtype)


def call(kernel, shapes, scratch, scalars, args, limit):
    vmem = pl.BlockSpec(memory_space=pltpu.VMEM)
    smem = pl.BlockSpec(memory_space=pltpu.SMEM)
    return pl.pallas_call(
        kernel,
        out_shape=shapes,
        in_specs=[smem] * len(scalars) + [vmem] * len(args),
        out_specs=jax.tree.map(lambda _: vmem, shapes),
        scratch_shapes=scratch,
        compiler_params=pltpu.CompilerParams(vmem_limit_bytes=limit * MIB),
    )(*scalars, *args)


def shape(*dims, dtype=jnp.float32):
    return jax.ShapeDtypeStruct(dims, dtype)


def spread(x, axis, groups=None):
    return lax.all_to_all(x, axis, 0, 0, tiled=True, axis_index_groups=groups)


def move(x, place):
    pairs = []
    for z in range(CHIPS):
        for c in range(CORES):
            to = place(z, c)
            pairs.append((z * CORES + c, to[0] % CHIPS * CORES + to[1]))
    return lax.ppermute(x, "row", pairs)


def ring(x):
    return move(x, lambda z, c: (z + 1 - 2 * c, c))


def partner(x):
    return move(x, lambda z, c: (z, 1 - c))


def held_order():
    table = []
    for z in range(CHIPS):
        for c in range(CORES):
            way = 2 * c - 1
            slots = [z * 2 + c, z * 2 + 1 - c]
            for k in range(1, CHIPS // 2):
                near, other = (z + way * k) % CHIPS, (z - way * k) % CHIPS
                slots += [near * 2 + c, near * 2 + 1 - c, other * 2 + 1 - c, other * 2 + c]
            across = (z + CHIPS // 2) % CHIPS
            table.append(slots + [across * 2 + c, across * 2 + 1 - c])
    table = jnp.asarray(np.array(table, np.int32))
    return lax.dynamic_index_in_dim(table, lax.axis_index("row"), 0, keepdims=False)


def gather_targets(target):
    held = jnp.concatenate([target, partner(target)])
    pieces = [held]
    for _ in range(1, CHIPS // 2):
        held = ring(held)
        pieces += [held, partner(held)]
    held = ring(held[: target.shape[0]])
    return pieces + [held, partner(held)]


def body(source, target, source_mass, target_mass, tile_src, tile_dst, tile_count):
    rows, cols = lax.axis_size("row"), lax.axis_size("col")
    width = source.shape[1]
    nsrc, ntgt = source_mass.shape[0] // BLK, target_mass.shape[0] // BLK
    src = spread(jnp.broadcast_to(source[None], (cols, *source.shape)), "col")
    src = src.reshape(-1, width)
    pieces = gather_targets(target)
    amass = source_mass.reshape(nsrc, BLK)
    bmass = target_mass.reshape(ntgt, BLK)
    order = held_order()
    scalars = (order, tile_src.reshape(-1), tile_dst.reshape(-1), tile_count.reshape(-1))
    far = pltpu.SMEM((nsrc * ntgt,), jnp.float32)

    def costs(first, some, last, held, outs):
        count = sum(piece.shape[0] for piece in some)
        return call(
            lambda *refs: cost_kernel(first, len(some), last, *refs),
            (shape(src.shape[0], count), *outs),
            [far],
            scalars,
            (src, *some, *held),
            24,
        )

    norms = shape(src.shape[0], BLK)
    cost_a, norm = costs(0, pieces[:5], False, (), (norms,))
    (cost_b,) = costs(10, pieces[5:7], False, (norm,), ())
    cost_c, part = costs(14, pieces[7:], True, (norm, cost_a, cost_b), (shape(cols, nsrc, BLK),))
    cost = (cost_a, cost_b, cost_c)

    for step in range(ITERS):
        fpot, part = call(
            target_kernel,
            (shape(nsrc, BLK), shape(rows, ntgt, BLK)),
            [pltpu.VMEM((src.shape[0], BLK), jnp.float32), pltpu.VMEM((ntgt, BLK), jnp.float32)],
            (order,),
            (spread(part, "col"), amass, *cost),
            16,
        )
        parts = spread(part, "row")
        if step < ITERS - 1:
            part = call(
                source_kernel,
                shape(cols, nsrc, BLK),
                [pltpu.VMEM((ntgt, BLK), jnp.float32)],
                (order,),
                (parts, bmass, *cost),
                16,
            )
    share = src.shape[0] // cols
    gpot, sums = call(
        lambda *refs: map_kernel(len(pieces), *refs),
        (shape(ntgt, BLK), shape(COLX, COLY * share, width + BLK, dtype=jnp.bfloat16)),
        [pltpu.VMEM((src.shape[0], ntgt * BLK), jnp.bfloat16)],
        (order,),
        (parts, bmass, fpot, *pieces, *cost),
        32,
    )
    xgroups = [[y * COLX + x for x in range(COLX)] for y in range(COLY)]
    ygroups = [[y * COLX + x for y in range(COLY)] for x in range(COLX)]
    sums = spread(sums, "col", xgroups)
    sums = call(add_kernel, shape(*sums.shape[1:], dtype=jnp.bfloat16), [], (), (sums,), 8)
    sums = spread(sums.reshape(COLY, share, -1), "col", ygroups)
    mapped = call(divide_kernel, shape(share, width, dtype=jnp.bfloat16), [], (), (sums,), 8)
    return (fpot.reshape(-1) * UNIT, gpot.reshape(-1) * UNIT, mapped)


def solution(mesh):
    in_specs = (
        P(("row", "col"), None),
        P(("col", "row"), None),
        P("row"),
        P("col"),
        P("row", "col", None),
        P("row", "col", None),
        P("row", "col"),
    )
    out_specs = (P("row"), P("col"), P(("row", "col"), None))
    return jax.shard_map(body, mesh=mesh, in_specs=in_specs, out_specs=out_specs, check_vma=False)
```

```python
import math

import jax
import jax.numpy as jnp
from jax import lax
from jax.experimental import pallas as pl
from jax.experimental.pallas import tpu as pltpu
from jax.sharding import PartitionSpec as P

BLK = 128
ITERS = 3
EPS = 0.02
UNIT = EPS * math.log(2.0)
FAR = 1e30
MIB = 1 << 20
CHIPS, CORES = 8, 2
CHUNK = 256


def nt_dot(a, b):
    return lax.dot_general(a, b, (((1,), (1,)), ((), ())), preferred_element_type=jnp.float32)


def square_sums(rows):
    rows = rows.astype(jnp.float32)
    rows = rows * rows
    total = rows[:, :BLK]
    for d in range(BLK, rows.shape[1], BLK):
        total = total + rows[:, d : d + BLK]
    return total


def lanes_of(row):
    return jnp.transpose(jnp.broadcast_to(row, (BLK, BLK)))


def finish_rows(peak, total):
    peak, total = jnp.transpose(peak), jnp.transpose(total)
    top = jnp.max(peak, axis=0, keepdims=True)
    return top + jnp.log2(jnp.sum(total * jnp.exp2(peak - top), axis=0, keepdims=True))


def tiles_of(cost_refs):
    return [(ref, slice(d, d + BLK)) for ref in cost_refs for d in range(0, ref.shape[1], BLK)]


def source_parts(cost_refs, pot_row, part_ref):
    tiles = tiles_of(cost_refs)
    for s in range(cost_refs[0].shape[0] // BLK):
        at = slice(s * BLK, (s + 1) * BLK)

        def gap(n):
            ref, lanes = tiles[n]
            return pot_row(n) - ref[at, lanes]

        peak = gap(0)
        for n in range(1, len(tiles)):
            peak = jnp.maximum(peak, gap(n))
        total = jnp.exp2(gap(0) - peak)
        for n in range(1, len(tiles)):
            total = total + jnp.exp2(gap(n) - peak)
        row = finish_rows(peak, total)
        for k in range(part_ref.shape[0]):
            part_ref[k, s : s + 1, :] = row


def cost_kernel(first, npiece, last, *refs):
    sidx, tidx, live, src_ref, *refs = refs
    order = held_order()
    pieces, refs = refs[:npiece], refs[npiece:]
    if first == 0:
        cost_ref, norm_ref, far = refs
    elif last:
        norm_ref, *held, cost_ref, part_ref, far = refs
    else:
        norm_ref, cost_ref, far = refs
    nsrc = src_ref.shape[0] // BLK
    ntgt = far.shape[0] // nsrc
    scale = 1.0 / (src_ref.shape[1] * UNIT)
    for i in range(far.shape[0]):
        far[i] = FAR

    def mark(k, c):
        far[sidx[k] * ntgt + tidx[k]] = 0.0
        return c

    lax.fori_loop(0, live[0], mark, 0)
    if first == 0:
        for s in range(nsrc):
            at = slice(s * BLK, (s + 1) * BLK)
            norm = jnp.sum(square_sums(src_ref[at, :]), axis=1, keepdims=True) * scale
            norm_ref[at, :] = jnp.broadcast_to(norm, (BLK, BLK))
    slot, lane = first, 0
    for piece in pieces:
        count = piece.shape[0] // BLK
        away = []
        for t in range(count):
            sums = jnp.transpose(square_sums(piece[t * BLK : (t + 1) * BLK, :]))
            away.append(jnp.sum(sums, axis=0, keepdims=True) * scale)
        cross = nt_dot(src_ref[...], piece[...]) * (-2.0 * scale)
        for s in range(nsrc):
            at = slice(s * BLK, (s + 1) * BLK)
            for t in range(count):
                far_off = far[s * ntgt + order[slot + t]]
                tile = cross[at, t * BLK : (t + 1) * BLK] + norm_ref[at, :] + (away[t] + far_off)
                cost_ref[at, lane + t * BLK : lane + (t + 1) * BLK] = tile
        slot += count
        lane += count * BLK
    if last:
        source_parts([*held, cost_ref], lambda n: 0.0, part_ref)


def combine(mass_ref, parts_ref):
    parts = parts_ref[...]
    top = jnp.max(parts, axis=0)
    low = jnp.log2(jnp.sum(jnp.exp2(parts - top[None]), axis=0))
    return jnp.log2(mass_ref[...]) - (top + low)


def target_kernel(parts_ref, mass_ref, *refs):
    *cost_refs, pot_ref, part_ref, wide, mine = refs
    order = held_order()
    pot = combine(mass_ref, parts_ref)
    pot_ref[...] = pot
    for s in range(pot.shape[0]):
        wide[s * BLK : (s + 1) * BLK, :] = lanes_of(pot[s : s + 1, :])
    for n, (ref, lanes) in enumerate(tiles_of(cost_refs)):
        gap = (wide[...] - ref[:, lanes]).reshape(-1, 8, BLK)
        peak = jnp.max(gap, axis=0)
        top = jnp.max(peak, axis=0, keepdims=True)
        total = jnp.sum(jnp.exp2(gap - top[None]), axis=0)
        mine[pl.ds(order[n], 1), :] = top + jnp.log2(jnp.sum(total, axis=0, keepdims=True))
    part_ref[...] = jnp.broadcast_to(mine[...][None], part_ref.shape)


def source_kernel(parts_ref, mass_ref, *refs):
    *cost_refs, part_ref, pot_ref = refs
    order = held_order()
    pot_ref[...] = combine(mass_ref, parts_ref)
    rows = [pot_ref[pl.ds(order[n], 1), :] for n in range(pot_ref.shape[0])]
    source_parts(cost_refs, lambda n: rows[n], part_ref)


def map_kernel(npiece, parts_ref, mass_ref, fpot_ref, *refs):
    pieces, refs = refs[:npiece], refs[npiece:]
    *cost_refs, fout_ref, gout_ref, sums_ref, pot_ref, weight = refs
    order = held_order()
    pot = combine(mass_ref, parts_ref)
    pot_ref[...] = pot
    gout_ref[...] = pot * UNIT
    fout_ref[...] = fpot_ref[...] * UNIT
    rows = [pot_ref[pl.ds(order[n], 1), :] for n in range(pot_ref.shape[0])]
    width = pieces[0].shape[1]
    for s in range(fpot_ref.shape[0]):
        at = slice(s * BLK, (s + 1) * BLK)
        mine = lanes_of(fpot_ref[s : s + 1, :])
        for n, (ref, lanes) in enumerate(tiles_of(cost_refs)):
            power = jnp.exp2(mine + rows[n] - ref[at, lanes])
            weight[at, n * BLK : (n + 1) * BLK] = power.astype(jnp.bfloat16)
    share = weight.shape[0] // sums_ref.shape[0]

    def put(block, lanes):
        for k in range(sums_ref.shape[0]):
            sums_ref[k, :, lanes] = block[k * share : (k + 1) * share, :]

    for d in range(0, width, CHUNK):
        part, lane = None, 0
        for piece in pieces:
            low = weight[:, lane : lane + piece.shape[0]]
            add = jnp.dot(low, piece[:, d : d + CHUNK], preferred_element_type=jnp.float32)
            part = add if part is None else part + add
            lane += piece.shape[0]
        put(part.astype(jnp.bfloat16), slice(d, d + CHUNK))
    ones = jnp.ones((weight.shape[1], BLK), jnp.bfloat16)
    total = jnp.dot(weight[...], ones, preferred_element_type=jnp.float32)
    put(two_pieces(total), slice(width, width + BLK))


def two_pieces(total):
    high = total.astype(jnp.bfloat16).astype(jnp.float32)
    lane = lax.broadcasted_iota(jnp.int32, total.shape, 1)
    return jnp.where(lane == 0, high, total - high).astype(jnp.bfloat16)


def add_up(sums_ref):
    sums = sums_ref[0].astype(jnp.float32)
    for k in range(1, sums_ref.shape[0]):
        sums = sums + sums_ref[k].astype(jnp.float32)
    return sums


def divide_kernel(sums_ref, out_ref):
    width = out_ref.shape[1]
    sums = add_up(sums_ref)
    total = sums[:, width : width + 1] + sums[:, width + 1 : width + 2]
    out_ref[...] = (sums[:, :width] / total).astype(out_ref.dtype)


def call(kernel, shapes, scratch, scalars, args, limit, flops=None):
    vmem = pl.BlockSpec(memory_space=pltpu.VMEM)
    smem = pl.BlockSpec(memory_space=pltpu.SMEM)
    return pl.pallas_call(
        kernel,
        out_shape=shapes,
        in_specs=[smem] * len(scalars) + [vmem] * len(args),
        out_specs=jax.tree.map(lambda _: vmem, shapes),
        scratch_shapes=scratch,
        compiler_params=pltpu.CompilerParams(vmem_limit_bytes=limit * MIB),
        cost_estimate=flops and pl.CostEstimate(flops=flops, bytes_accessed=0, transcendentals=0),
    )(*scalars, *args)


def shape(*dims, dtype=jnp.float32):
    return jax.ShapeDtypeStruct(dims, dtype)


def spread(x, axis, groups=None):
    return lax.all_to_all(x, axis, 0, 0, tiled=True, axis_index_groups=groups)


def move(x, place):
    pairs = []
    for z in range(CHIPS):
        for c in range(CORES):
            to = place(z, c)
            pairs.append((z * CORES + c, to[0] % CHIPS * CORES + to[1]))
    return lax.ppermute(x, "row", pairs)


def ring(x):
    return move(x, lambda z, c: (z + 1 - 2 * c, c))


def partner(x):
    return move(x, lambda z, c: (z, 1 - c))


def held_order():
    row = lax.axis_index("row")
    z, c = row // CORES, row % CORES
    way = 2 * c - 1
    slots = [z * 2 + c, z * 2 + 1 - c]
    for k in range(1, CHIPS // 2):
        near, other = (z + way * k + CHIPS) % CHIPS, (z - way * k + CHIPS) % CHIPS
        slots += [near * 2 + c, near * 2 + 1 - c, other * 2 + 1 - c, other * 2 + c]
    across = (z + CHIPS // 2) % CHIPS
    return slots + [across * 2 + c, across * 2 + 1 - c]


def body(source, target, source_mass, target_mass, tile_src, tile_dst, tile_count):
    rows, cols = lax.axis_size("row"), lax.axis_size("col")
    width = source.shape[1]
    nsrc, ntgt = source_mass.shape[0] // BLK, target_mass.shape[0] // BLK
    src = spread(jnp.broadcast_to(source[None], (cols, *source.shape)), "col")
    src = src.reshape(-1, width)
    amass = source_mass.reshape(nsrc, BLK)
    bmass = target_mass.reshape(ntgt, BLK)
    scalars = (tile_src.reshape(-1), tile_dst.reshape(-1), tile_count.reshape(-1))

    def costs(first, some, last, held, outs):
        count = sum(piece.shape[0] for piece in some)
        return call(
            lambda *refs: cost_kernel(first, len(some), last, *refs),
            (shape(src.shape[0], count), *outs),
            [pltpu.SMEM((nsrc * ntgt,), jnp.float32)],
            scalars,
            (src, *some, *held),
            24,
            2 * src.shape[0] * count * width,
        )

    held = [jnp.concatenate([target, partner(target)])]
    for _ in range(1, CHIPS // 2):
        held.append(ring(held[-1]))
    others = [partner(block) for block in held[1:]]
    cost_a, norm = costs(
        0, (held[0], held[1], others[0], held[2], others[1]), False, (), (shape(src.shape[0], BLK),)
    )
    (cost_b,) = costs(10, (held[3], others[2]), False, (norm,), ())
    held.append(ring(held[3][: target.shape[0]]))
    held[4], cost_a = lax.optimization_barrier((held[4], cost_a))
    others.append(partner(held[4]))
    cost_c, part = costs(
        14, (held[4], others[3]), True, (norm, cost_a, cost_b), (shape(cols, nsrc, BLK),)
    )
    cost = (cost_a, cost_b, cost_c)
    pieces = [held[0]]
    for block, other in zip(held[1:], others):
        pieces += [block, other]

    for step in range(ITERS):
        fpot, part = call(
            target_kernel,
            (shape(nsrc, BLK), shape(rows, ntgt, BLK)),
            [pltpu.VMEM((src.shape[0], BLK), jnp.float32), pltpu.VMEM((ntgt, BLK), jnp.float32)],
            (),
            (spread(part, "col"), amass, *cost),
            16,
        )
        parts = spread(part, "row")
        if step < ITERS - 1:
            part = call(
                source_kernel,
                shape(cols, nsrc, BLK),
                [pltpu.VMEM((ntgt, BLK), jnp.float32)],
                (),
                (parts, bmass, *cost),
                16,
            )
    share = src.shape[0] // cols
    fout, gout, sums = call(
        lambda *refs: map_kernel(len(pieces), *refs),
        (shape(nsrc, BLK), shape(ntgt, BLK), shape(cols, share, width + BLK, dtype=jnp.bfloat16)),
        [
            pltpu.VMEM((ntgt, BLK), jnp.float32),
            pltpu.VMEM((src.shape[0], ntgt * BLK), jnp.bfloat16),
        ],
        (),
        (parts, bmass, fpot, *pieces, *cost),
        24,
    )
    sums = spread(sums, "col")
    mapped = call(divide_kernel, shape(share, width, dtype=jnp.bfloat16), [], (), (sums,), 8)
    return (fout.reshape(-1), gout.reshape(-1), mapped)


def solution(mesh):
    in_specs = (
        P(("row", "col"), None),
        P(("col", "row"), None),
        P("row"),
        P("col"),
        P("row", "col", None),
        P("row", "col", None),
        P("row", "col"),
    )
    out_specs = (P("row"), P("col"), P(("row", "col"), None))
    return jax.shard_map(body, mesh=mesh, in_specs=in_specs, out_specs=out_specs, check_vma=False)
```

```python
import math

import jax
import jax.numpy as jnp
from jax import lax
from jax.experimental import pallas as pl
from jax.experimental.pallas import tpu as pltpu
from jax.sharding import PartitionSpec as P

BLK = 128
ITERS = 3
EPS = 0.02
UNIT = EPS * math.log(2.0)
FAR = 1e30
MIB = 1 << 20
CHUNK = 256


def nt_dot(a, b):
    return lax.dot_general(a, b, (((1,), (1,)), ((), ())), preferred_element_type=jnp.float32)


def square_sums(rows):
    rows = rows.astype(jnp.float32)
    rows = rows * rows
    total = rows[:, :BLK]
    for d in range(BLK, rows.shape[1], BLK):
        total = total + rows[:, d : d + BLK]
    return total


def lanes_of(row):
    return jnp.transpose(jnp.broadcast_to(row, (BLK, BLK)))


def finish_rows(peak, total):
    peak, total = jnp.transpose(peak), jnp.transpose(total)
    top = jnp.max(peak, axis=0, keepdims=True)
    return top + jnp.log2(jnp.sum(total * jnp.exp2(peak - top), axis=0, keepdims=True))


def source_parts(cost_ref, pot, part_ref):
    count = cost_ref.shape[1] // BLK
    for s in range(cost_ref.shape[0] // BLK):
        at = slice(s * BLK, (s + 1) * BLK)

        def gap(n):
            cost = cost_ref[at, n * BLK : (n + 1) * BLK]
            return -cost if pot is None else pot[n : n + 1, :] - cost

        peak = gap(0)
        for n in range(1, count):
            peak = jnp.maximum(peak, gap(n))
        total = jnp.exp2(gap(0) - peak)
        for n in range(1, count):
            total = total + jnp.exp2(gap(n) - peak)
        row = finish_rows(peak, total)
        for k in range(part_ref.shape[0]):
            part_ref[k, s : s + 1, :] = row


def prepare_kernel(sidx, tidx, live, src_ref, norm_ref, far_ref):
    nsrc = src_ref.shape[0] // BLK
    ntgt = far_ref.shape[0] // nsrc
    scale = 1.0 / (src_ref.shape[1] * UNIT)
    far_ref[...] = jnp.full_like(far_ref, FAR)

    def mark(k, c):
        far_ref[pl.ds(sidx[k] * ntgt + tidx[k], 1), :] = jnp.zeros((1, BLK), jnp.float32)
        return c

    lax.fori_loop(0, live[0], mark, 0)
    for s in range(nsrc):
        at = slice(s * BLK, (s + 1) * BLK)
        norm = jnp.sum(square_sums(src_ref[at, :]), axis=1, keepdims=True) * scale
        norm_ref[at, :] = jnp.broadcast_to(norm, (BLK, BLK))


def cost_kernel(src_ref, norm_ref, far_ref, tgt_ref, cost_ref, part_ref, tgt, sems):
    nsrc, ntgt = src_ref.shape[0] // BLK, tgt_ref.shape[0] // BLK
    scale = 1.0 / (src_ref.shape[1] * UNIT)
    chunks = tgt_ref.shape[0] // CHUNK

    def chunk(k):
        at = pl.ds(k * CHUNK, CHUNK)
        return pltpu.make_async_copy(tgt_ref.at[at, :], tgt.at[at, :], sems.at[k])

    for k in range(chunks):
        chunk(k).start()
    for k in range(chunks):
        chunk(k).wait()
        cross = nt_dot(src_ref[...], tgt[k * CHUNK : (k + 1) * CHUNK, :]) * (-2.0 * scale)
        for d in range(0, CHUNK, BLK):
            lane = k * CHUNK + d
            sums = jnp.transpose(square_sums(tgt[lane : lane + BLK, :]))
            norm = jnp.sum(sums, axis=0, keepdims=True) * scale
            for s in range(nsrc):
                at = slice(s * BLK, (s + 1) * BLK)
                n = s * ntgt + lane // BLK
                away = norm + far_ref[n : n + 1, :]
                cost_ref[at, lane : lane + BLK] = cross[at, d : d + BLK] + norm_ref[at, :] + away
    source_parts(cost_ref, None, part_ref)


def combine(mass_ref, parts_ref):
    parts = parts_ref[...]
    top = jnp.max(parts, axis=0)
    low = jnp.log2(jnp.sum(jnp.exp2(parts - top[None]), axis=0))
    return jnp.log2(mass_ref[...]) - (top + low)


def target_kernel(parts_ref, mass_ref, cost_ref, pot_ref, part_ref, wide, mine):
    pot = combine(mass_ref, parts_ref)
    pot_ref[...] = pot
    for s in range(pot.shape[0]):
        wide[s * BLK : (s + 1) * BLK, :] = lanes_of(pot[s : s + 1, :])
    for n in range(cost_ref.shape[1] // BLK):
        gap = (wide[...] - cost_ref[:, n * BLK : (n + 1) * BLK]).reshape(-1, 8, BLK)
        peak = jnp.max(gap, axis=0)
        top = jnp.max(peak, axis=0, keepdims=True)
        total = jnp.sum(jnp.exp2(gap - top[None]), axis=0)
        mine[n : n + 1, :] = top + jnp.log2(jnp.sum(total, axis=0, keepdims=True))
    part_ref[...] = jnp.broadcast_to(mine[...][None], part_ref.shape)


def source_kernel(parts_ref, mass_ref, cost_ref, part_ref):
    source_parts(cost_ref, combine(mass_ref, parts_ref), part_ref)


def map_kernel(parts_ref, mass_ref, fpot_ref, tgt_ref, cost_ref, pot_ref, sums_ref, weight):
    pot = combine(mass_ref, parts_ref)
    pot_ref[...] = pot
    width = tgt_ref.shape[1]
    for s in range(fpot_ref.shape[0]):
        at = slice(s * BLK, (s + 1) * BLK)
        mine = lanes_of(fpot_ref[s : s + 1, :])
        for n in range(pot.shape[0]):
            lanes = slice(n * BLK, (n + 1) * BLK)
            power = jnp.exp2(mine + pot[n : n + 1, :] - cost_ref[at, lanes])
            weight[at, lanes] = power.astype(jnp.bfloat16)
    for d in range(0, width, CHUNK):
        part = jnp.dot(weight[...], tgt_ref[:, d : d + CHUNK], preferred_element_type=jnp.float32)
        sums_ref[:, d : d + CHUNK] = part.astype(jnp.bfloat16)
    ones = jnp.ones((weight.shape[1], BLK), jnp.bfloat16)
    total = jnp.dot(weight[...], ones, preferred_element_type=jnp.float32)
    sums_ref[:, width:] = two_pieces(total)


def two_pieces(total):
    high = total.astype(jnp.bfloat16).astype(jnp.float32)
    lane = lax.broadcasted_iota(jnp.int32, total.shape, 1)
    return jnp.where(lane == 0, high, total - high).astype(jnp.bfloat16)


def add_up(sums_ref):
    sums = sums_ref[0].astype(jnp.float32)
    for k in range(1, sums_ref.shape[0]):
        sums = sums + sums_ref[k].astype(jnp.float32)
    return sums


def divide_kernel(sums_ref, out_ref):
    width = out_ref.shape[1]
    sums = add_up(sums_ref)
    total = sums[:, width : width + 1] + sums[:, width + 1 : width + 2]
    out_ref[...] = (sums[:, :width] / total).astype(out_ref.dtype)


def call(kernel, shapes, scratch, args, limit, specs=None):
    vmem = pl.BlockSpec(memory_space=pltpu.VMEM)
    return pl.pallas_call(
        kernel,
        out_shape=shapes,
        in_specs=specs or [vmem] * len(args),
        out_specs=jax.tree.map(lambda _: vmem, shapes),
        scratch_shapes=scratch,
        compiler_params=pltpu.CompilerParams(vmem_limit_bytes=limit * MIB),
    )(*args)


def shape(*dims, dtype=jnp.float32):
    return jax.ShapeDtypeStruct(dims, dtype)


def spread(x, axis):
    return lax.all_to_all(x, axis, 0, 0, tiled=True)


def body(source, target, source_mass, target_mass, tile_src, tile_dst, tile_count):
    rows, cols = lax.axis_size("row"), lax.axis_size("col")
    width = source.shape[1]
    tgt = lax.all_gather(target, "row", axis=0, tiled=True)
    src = spread(jnp.broadcast_to(source[None], (cols, *source.shape)), "col")
    src = src.reshape(-1, width)
    nsrc, ntgt = src.shape[0] // BLK, tgt.shape[0] // BLK
    amass = source_mass.reshape(nsrc, BLK)
    bmass = target_mass.reshape(ntgt, BLK)
    vmem, smem = (pl.BlockSpec(memory_space=space) for space in (pltpu.VMEM, pltpu.SMEM))
    norm, far = call(
        prepare_kernel,
        (shape(src.shape[0], BLK), shape(nsrc * ntgt, BLK)),
        [],
        (tile_src.reshape(-1), tile_dst.reshape(-1), tile_count.reshape(-1), src),
        8,
        [smem, smem, smem, vmem],
    )
    cost, part = call(
        cost_kernel,
        (shape(src.shape[0], tgt.shape[0]), shape(cols, nsrc, BLK)),
        [pltpu.VMEM(tgt.shape, tgt.dtype), pltpu.SemaphoreType.DMA((tgt.shape[0] // CHUNK,))],
        (src, norm, far, tgt),
        46,
        [vmem, vmem, vmem, pl.BlockSpec(memory_space=pl.ANY)],
    )
    for step in range(ITERS):
        fpot, part = call(
            target_kernel,
            (shape(nsrc, BLK), shape(rows, ntgt, BLK)),
            [pltpu.VMEM((src.shape[0], BLK), jnp.float32), pltpu.VMEM((ntgt, BLK), jnp.float32)],
            (spread(part, "col"), amass, cost),
            16,
        )
        parts = spread(part, "row")
        if step < ITERS - 1:
            part = call(source_kernel, shape(cols, nsrc, BLK), [], (parts, bmass, cost), 16)
    gpot, sums = call(
        map_kernel,
        (shape(ntgt, BLK), shape(src.shape[0], width + BLK, dtype=jnp.bfloat16)),
        [pltpu.VMEM(cost.shape, jnp.bfloat16)],
        (parts, bmass, fpot, tgt, cost),
        32,
    )
    share = src.shape[0] // cols
    sums = spread(sums.reshape(cols, share, -1), "col")
    mapped = call(divide_kernel, shape(share, width, dtype=jnp.bfloat16), [], (sums,), 8)
    return (fpot.reshape(-1) * UNIT, gpot.reshape(-1) * UNIT, mapped)


def solution(mesh):
    in_specs = (
        P(("row", "col"), None),
        P(("col", "row"), None),
        P("row"),
        P("col"),
        P("row", "col", None),
        P("row", "col", None),
        P("row", "col"),
    )
    out_specs = (P("row"), P("col"), P(("row", "col"), None))
    return jax.shard_map(body, mesh=mesh, in_specs=in_specs, out_specs=out_specs, check_vma=False)
```

```python
import math

import jax
import jax.numpy as jnp
from jax import lax
from jax.experimental import pallas as pl
from jax.experimental.pallas import tpu as pltpu
from jax.sharding import PartitionSpec as P

BLK = 128
ITERS = 3
EPS = 0.02
UNIT = EPS * math.log(2.0)
FAR = 1e30
MIB = 1 << 20
CHIPS, CORES = 8, 2
CHUNK = 256


def nt_dot(a, b):
    return lax.dot_general(a, b, (((1,), (1,)), ((), ())), preferred_element_type=jnp.float32)


def square_sums(rows):
    rows = rows.astype(jnp.float32)
    rows = rows * rows
    total = rows[:, :BLK]
    for d in range(BLK, rows.shape[1], BLK):
        total = total + rows[:, d : d + BLK]
    return total


def lanes_of(row):
    return jnp.transpose(jnp.broadcast_to(row, (BLK, BLK)))


def finish_rows(peak, total):
    peak, total = jnp.transpose(peak), jnp.transpose(total)
    top = jnp.max(peak, axis=0, keepdims=True)
    return top + jnp.log2(jnp.sum(total * jnp.exp2(peak - top), axis=0, keepdims=True))


def tiles_of(cost_refs):
    return [(ref, slice(d, d + BLK)) for ref in cost_refs for d in range(0, ref.shape[1], BLK)]


def source_parts(cost_refs, rows, part_ref):
    tiles = tiles_of(cost_refs)
    for s in range(cost_refs[0].shape[0] // BLK):
        at = slice(s * BLK, (s + 1) * BLK)

        def gap(n):
            ref, lanes = tiles[n]
            return -ref[at, lanes] if rows is None else rows[n] - ref[at, lanes]

        peak = gap(0)
        for n in range(1, len(tiles)):
            peak = jnp.maximum(peak, gap(n))
        total = jnp.exp2(gap(0) - peak)
        for n in range(1, len(tiles)):
            total = total + jnp.exp2(gap(n) - peak)
        row = finish_rows(peak, total)
        for k in range(part_ref.shape[0]):
            part_ref[k, s : s + 1, :] = row


def prepare_kernel(sidx, tidx, live, src_ref, norm_ref, far_ref, slot):
    nsrc = src_ref.shape[0] // BLK
    ntgt = far_ref.shape[0] // nsrc
    scale = 1.0 / (src_ref.shape[1] * UNIT)
    for n, cluster in enumerate(held_order()):
        slot[cluster] = n
    far_ref[...] = jnp.full_like(far_ref, FAR)

    def mark(k, c):
        far_ref[pl.ds(sidx[k] * ntgt + slot[tidx[k]], 1), :] = jnp.zeros((1, BLK), jnp.float32)
        return c

    lax.fori_loop(0, live[0], mark, 0)
    for s in range(nsrc):
        at = slice(s * BLK, (s + 1) * BLK)
        norm = jnp.sum(square_sums(src_ref[at, :]), axis=1, keepdims=True) * scale
        norm_ref[at, :] = jnp.broadcast_to(norm, (BLK, BLK))


def cost_kernel(first, npiece, nheld, src_ref, norm_ref, far_ref, *refs):
    pieces, held, (cost_ref, *more) = refs[:npiece], refs[npiece : npiece + nheld], refs[npiece + nheld :]
    nsrc = src_ref.shape[0] // BLK
    ntgt = far_ref.shape[0] // nsrc
    scale = 1.0 / (src_ref.shape[1] * UNIT)
    lane = 0
    for piece in pieces:
        for row in range(0, piece.shape[0], CHUNK):
            block = piece[row : row + CHUNK, :]
            cross = nt_dot(src_ref[...], block) * (-2.0 * scale)
            for d in range(0, block.shape[0], BLK):
                sums = jnp.transpose(square_sums(block[d : d + BLK, :]))
                norm = jnp.sum(sums, axis=0, keepdims=True) * scale
                for s in range(nsrc):
                    at = slice(s * BLK, (s + 1) * BLK)
                    n = s * ntgt + first + lane // BLK
                    away = norm + far_ref[n : n + 1, :]
                    tile = cross[at, d : d + BLK] + norm_ref[at, :] + away
                    cost_ref[at, lane : lane + BLK] = tile
                lane += BLK
    if more:
        source_parts([*held, cost_ref], None, more[0])


def combine(mass_ref, parts_ref):
    parts = parts_ref[...]
    top = jnp.max(parts, axis=0)
    low = jnp.log2(jnp.sum(jnp.exp2(parts - top[None]), axis=0))
    return jnp.log2(mass_ref[...]) - (top + low)


def target_kernel(parts_ref, mass_ref, *refs):
    *cost_refs, pot_ref, part_ref, wide, mine = refs
    order = held_order()
    pot = combine(mass_ref, parts_ref)
    pot_ref[...] = pot
    for s in range(pot.shape[0]):
        wide[s * BLK : (s + 1) * BLK, :] = lanes_of(pot[s : s + 1, :])
    for n, (ref, lanes) in enumerate(tiles_of(cost_refs)):
        gap = (wide[...] - ref[:, lanes]).reshape(-1, 8, BLK)
        peak = jnp.max(gap, axis=0)
        top = jnp.max(peak, axis=0, keepdims=True)
        total = jnp.sum(jnp.exp2(gap - top[None]), axis=0)
        mine[pl.ds(order[n], 1), :] = top + jnp.log2(jnp.sum(total, axis=0, keepdims=True))
    part_ref[...] = jnp.broadcast_to(mine[...][None], part_ref.shape)


def held_rows(pot_ref):
    return [pot_ref[pl.ds(cluster, 1), :] for cluster in held_order()]


def source_kernel(parts_ref, mass_ref, *refs):
    *cost_refs, part_ref, pot_ref = refs
    pot_ref[...] = combine(mass_ref, parts_ref)
    source_parts(cost_refs, held_rows(pot_ref), part_ref)


def map_kernel(npiece, parts_ref, mass_ref, fpot_ref, *refs):
    pieces, (*cost_refs, pot_ref, sums_ref, weight) = refs[:npiece], refs[npiece:]
    pot_ref[...] = combine(mass_ref, parts_ref)
    rows = held_rows(pot_ref)
    width = pieces[0].shape[1]
    for s in range(fpot_ref.shape[0]):
        at = slice(s * BLK, (s + 1) * BLK)
        mine = lanes_of(fpot_ref[s : s + 1, :])
        for n, (ref, lanes) in enumerate(tiles_of(cost_refs)):
            power = jnp.exp2(mine + rows[n] - ref[at, lanes])
            weight[at, n * BLK : (n + 1) * BLK] = power.astype(jnp.bfloat16)
    for d in range(0, width, CHUNK):
        part, lane = None, 0
        for piece in pieces:
            low = weight[:, lane : lane + piece.shape[0]]
            add = jnp.dot(low, piece[:, d : d + CHUNK], preferred_element_type=jnp.float32)
            part = add if part is None else part + add
            lane += piece.shape[0]
        sums_ref[:, d : d + CHUNK] = part.astype(jnp.bfloat16)
    ones = jnp.ones((weight.shape[1], BLK), jnp.bfloat16)
    total = jnp.dot(weight[...], ones, preferred_element_type=jnp.float32)
    sums_ref[:, width:] = two_pieces(total)


def two_pieces(total):
    high = total.astype(jnp.bfloat16).astype(jnp.float32)
    lane = lax.broadcasted_iota(jnp.int32, total.shape, 1)
    return jnp.where(lane == 0, high, total - high).astype(jnp.bfloat16)


def add_up(sums_ref):
    sums = sums_ref[0].astype(jnp.float32)
    for k in range(1, sums_ref.shape[0]):
        sums = sums + sums_ref[k].astype(jnp.float32)
    return sums


def divide_kernel(sums_ref, out_ref):
    width = out_ref.shape[1]
    sums = add_up(sums_ref)
    total = sums[:, width : width + 1] + sums[:, width + 1 : width + 2]
    out_ref[...] = (sums[:, :width] / total).astype(out_ref.dtype)


def call(kernel, shapes, scratch, args, limit, specs=None):
    vmem = pl.BlockSpec(memory_space=pltpu.VMEM)
    return pl.pallas_call(
        kernel,
        out_shape=shapes,
        in_specs=specs or [vmem] * len(args),
        out_specs=jax.tree.map(lambda _: vmem, shapes),
        scratch_shapes=scratch,
        compiler_params=pltpu.CompilerParams(vmem_limit_bytes=limit * MIB),
    )(*args)


def shape(*dims, dtype=jnp.float32):
    return jax.ShapeDtypeStruct(dims, dtype)


def spread(x, axis):
    return lax.all_to_all(x, axis, 0, 0, tiled=True)


def move(x, place):
    pairs = []
    for z in range(CHIPS):
        for c in range(CORES):
            to = place(z, c)
            pairs.append((z * CORES + c, to[0] % CHIPS * CORES + to[1]))
    return lax.ppermute(x, "row", pairs)


def ring(x):
    return move(x, lambda z, c: (z + 1 - 2 * c, c))


def partner(x):
    return move(x, lambda z, c: (z, 1 - c))


def held_order():
    row = lax.axis_index("row")
    z, c = row // CORES, row % CORES
    way = 2 * c - 1

    def pair(k, core):
        chip = (z + way * k + CHIPS) % CHIPS
        return [chip * CORES + core, chip * CORES + 1 - core]

    return [
        *pair(0, c),
        *pair(1, c),
        *pair(2, c),
        *pair(-1, 1 - c),
        *pair(-2, 1 - c),
        *pair(3, c),
        *pair(-3, 1 - c),
        *pair(4, c),
    ]


def body(source, target, source_mass, target_mass, tile_src, tile_dst, tile_count):
    rows, cols = lax.axis_size("row"), lax.axis_size("col")
    width = source.shape[1]
    nsrc, ntgt = source_mass.shape[0] // BLK, target_mass.shape[0] // BLK
    near = partner(target)
    one, near_one = ring(target), ring(near)
    src = spread(jnp.broadcast_to(source[None], (cols, *source.shape)), "col")
    src = src.reshape(-1, width)
    two, near_two = ring(one), ring(near_one)
    three, near_three = ring(two), ring(near_two)
    own = jnp.concatenate([target, near])
    early = jnp.concatenate([one, near_one, two, near_two])
    late = jnp.concatenate([three, near_three])
    early_other = partner(early)
    last = ring(three)
    late_other = partner(late)
    amass = source_mass.reshape(nsrc, BLK)
    bmass = target_mass.reshape(ntgt, BLK)
    vmem, smem = (pl.BlockSpec(memory_space=space) for space in (pltpu.VMEM, pltpu.SMEM))
    norm, far = call(
        prepare_kernel,
        (shape(src.shape[0], BLK), shape(nsrc * ntgt, BLK)),
        [pltpu.SMEM((ntgt,), jnp.int32)],
        (tile_src.reshape(-1), tile_dst.reshape(-1), tile_count.reshape(-1), src),
        8,
        [smem, smem, smem, vmem],
    )

    def costs(first, some, held=(), outs=()):
        return call(
            lambda *refs: cost_kernel(first, len(some), len(held), *refs),
            (shape(src.shape[0], sum(piece.shape[0] for piece in some)), *outs),
            [],
            (src, norm, far, *some, *held),
            12,
        )

    (cost_a,) = costs(0, (own, early, early_other))
    (cost_b,) = costs(10, (late, late_other))
    last, cost_a = lax.optimization_barrier((last, cost_a))
    last_other = partner(last)
    cost_c, part = costs(14, (last, last_other), (cost_a, cost_b), (shape(cols, nsrc, BLK),))
    cost = (cost_a, cost_b, cost_c)
    pieces = (own, early, early_other, late, late_other, last, last_other)

    for step in range(ITERS):
        fpot, part = call(
            target_kernel,
            (shape(nsrc, BLK), shape(rows, ntgt, BLK)),
            [pltpu.VMEM((src.shape[0], BLK), jnp.float32), pltpu.VMEM((ntgt, BLK), jnp.float32)],
            (spread(part, "col"), amass, *cost),
            12,
        )
        parts = spread(part, "row")
        if step < ITERS - 1:
            part = call(
                source_kernel,
                shape(cols, nsrc, BLK),
                [pltpu.VMEM((ntgt, BLK), jnp.float32)],
                (parts, bmass, *cost),
                12,
            )
    gpot, sums = call(
        lambda *refs: map_kernel(len(pieces), *refs),
        (shape(ntgt, BLK), shape(src.shape[0], width + BLK, dtype=jnp.bfloat16)),
        [pltpu.VMEM((src.shape[0], ntgt * BLK), jnp.bfloat16)],
        (parts, bmass, fpot, *pieces, *cost),
        18,
    )
    share = src.shape[0] // cols
    sums = spread(sums.reshape(cols, share, -1), "col")
    mapped = call(divide_kernel, shape(share, width, dtype=jnp.bfloat16), [], (sums,), 8)
    return (fpot.reshape(-1) * UNIT, gpot.reshape(-1) * UNIT, mapped)


def solution(mesh):
    in_specs = (
        P(("row", "col"), None),
        P(("col", "row"), None),
        P("row"),
        P("col"),
        P("row", "col", None),
        P("row", "col", None),
        P("row", "col"),
    )
    out_specs = (P("row"), P("col"), P(("row", "col"), None))
    return jax.shard_map(body, mesh=mesh, in_specs=in_specs, out_specs=out_specs, check_vma=False)
```

```python
import math

import jax
import jax.numpy as jnp
from jax import lax
from jax.experimental import pallas as pl
from jax.experimental.pallas import tpu as pltpu
from jax.sharding import PartitionSpec as P

BLK = 128
ITERS = 3
EPS = 0.02
UNIT = EPS * math.log(2.0)
FAR = 1e30
MIB = 1 << 20
CHIPS, CORES = 8, 2
CHUNK = 256


def nt_dot(a, b):
    return lax.dot_general(a, b, (((1,), (1,)), ((), ())), preferred_element_type=jnp.float32)


def square_sums(rows):
    rows = rows.astype(jnp.float32)
    rows = rows * rows
    total = rows[:, :BLK]
    for d in range(BLK, rows.shape[1], BLK):
        total = total + rows[:, d : d + BLK]
    return total


def lanes_of(row):
    return jnp.transpose(jnp.broadcast_to(row, (BLK, BLK)))


def finish_rows(peak, total):
    peak, total = jnp.transpose(peak), jnp.transpose(total)
    top = jnp.max(peak, axis=0, keepdims=True)
    return top + jnp.log2(jnp.sum(total * jnp.exp2(peak - top), axis=0, keepdims=True))


def tiles_of(cost_refs):
    return [(ref, slice(d, d + BLK)) for ref in cost_refs for d in range(0, ref.shape[1], BLK)]


def source_parts(cost_refs, rows, part_ref):
    tiles = tiles_of(cost_refs)
    for s in range(cost_refs[0].shape[0] // BLK):
        at = slice(s * BLK, (s + 1) * BLK)

        def gap(n):
            ref, lanes = tiles[n]
            return -ref[at, lanes] if rows is None else rows[n] - ref[at, lanes]

        peak = gap(0)
        for n in range(1, len(tiles)):
            peak = jnp.maximum(peak, gap(n))
        total = jnp.exp2(gap(0) - peak)
        for n in range(1, len(tiles)):
            total = total + jnp.exp2(gap(n) - peak)
        row = finish_rows(peak, total)
        for k in range(part_ref.shape[0]):
            part_ref[k, s : s + 1, :] = row


def prepare_kernel(sidx, tidx, live, src_ref, norm_ref, far_ref, slot):
    nsrc = src_ref.shape[0] // BLK
    ntgt = far_ref.shape[0] // nsrc
    scale = 1.0 / (src_ref.shape[1] * UNIT)
    for n, cluster in enumerate(held_order()):
        slot[cluster] = n
    far_ref[...] = jnp.full_like(far_ref, FAR)

    def mark(k, c):
        far_ref[pl.ds(sidx[k] * ntgt + slot[tidx[k]], 1), :] = jnp.zeros((1, BLK), jnp.float32)
        return c

    lax.fori_loop(0, live[0], mark, 0)
    for s in range(nsrc):
        at = slice(s * BLK, (s + 1) * BLK)
        norm = jnp.sum(square_sums(src_ref[at, :]), axis=1, keepdims=True) * scale
        norm_ref[at, :] = jnp.broadcast_to(norm, (BLK, BLK))


def cost_kernel(first, npiece, nheld, src_ref, norm_ref, far_ref, *refs):
    pieces, held, (cost_ref, *more) = refs[:npiece], refs[npiece : npiece + nheld], refs[npiece + nheld :]
    nsrc = src_ref.shape[0] // BLK
    ntgt = far_ref.shape[0] // nsrc
    scale = 1.0 / (src_ref.shape[1] * UNIT)
    lane = 0
    for piece in pieces:
        for row in range(0, piece.shape[0], CHUNK):
            block = piece[row : row + CHUNK, :]
            cross = nt_dot(src_ref[...], block) * (-2.0 * scale)
            for d in range(0, block.shape[0], BLK):
                sums = jnp.transpose(square_sums(block[d : d + BLK, :]))
                norm = jnp.sum(sums, axis=0, keepdims=True) * scale
                for s in range(nsrc):
                    at = slice(s * BLK, (s + 1) * BLK)
                    n = s * ntgt + first + lane // BLK
                    away = norm + far_ref[n : n + 1, :]
                    tile = cross[at, d : d + BLK] + norm_ref[at, :] + away
                    cost_ref[at, lane : lane + BLK] = tile
                lane += BLK
    if more:
        source_parts([*held, cost_ref], None, more[0])


def combine(mass_ref, parts_ref):
    parts = parts_ref[...]
    top = jnp.max(parts, axis=0)
    low = jnp.log2(jnp.sum(jnp.exp2(parts - top[None]), axis=0))
    return jnp.log2(mass_ref[...]) - (top + low)


def target_kernel(parts_ref, mass_ref, *refs):
    *cost_refs, pot_ref, part_ref, wide, held, mine = refs
    pot = combine(mass_ref, parts_ref)
    pot_ref[...] = pot
    for s in range(pot.shape[0]):
        wide[s * BLK : (s + 1) * BLK, :] = lanes_of(pot[s : s + 1, :])
    for n, (ref, lanes) in enumerate(tiles_of(cost_refs)):
        gap = (wide[...] - ref[:, lanes]).reshape(-1, 8, BLK)
        peak = jnp.max(gap, axis=0)
        top = jnp.max(peak, axis=0, keepdims=True)
        total = jnp.sum(jnp.exp2(gap - top[None]), axis=0)
        held[n : n + 1, :] = top + jnp.log2(jnp.sum(total, axis=0, keepdims=True))
    for cluster, slot in enumerate(held_slots()):
        mine[cluster : cluster + 1, :] = held[pl.ds(slot, 1), :]
    part_ref[...] = jnp.broadcast_to(mine[...][None], part_ref.shape)


def held_rows(pot_ref):
    return [pot_ref[pl.ds(cluster, 1), :] for cluster in held_order()]


def source_kernel(parts_ref, mass_ref, *refs):
    *cost_refs, part_ref, pot_ref = refs
    pot_ref[...] = combine(mass_ref, parts_ref)
    source_parts(cost_refs, held_rows(pot_ref), part_ref)


def map_kernel(npiece, parts_ref, mass_ref, fpot_ref, *refs):
    pieces, (*cost_refs, pot_ref, sums_ref, weight) = refs[:npiece], refs[npiece:]
    pot_ref[...] = combine(mass_ref, parts_ref)
    rows = held_rows(pot_ref)
    width = pieces[0].shape[1]
    for s in range(fpot_ref.shape[0]):
        at = slice(s * BLK, (s + 1) * BLK)
        mine = lanes_of(fpot_ref[s : s + 1, :])
        for n, (ref, lanes) in enumerate(tiles_of(cost_refs)):
            power = jnp.exp2(mine + rows[n] - ref[at, lanes])
            weight[at, n * BLK : (n + 1) * BLK] = power.astype(jnp.bfloat16)
    for d in range(0, width, CHUNK):
        part, lane = None, 0
        for piece in pieces:
            low = weight[:, lane : lane + piece.shape[0]]
            add = jnp.dot(low, piece[:, d : d + CHUNK], preferred_element_type=jnp.float32)
            part = add if part is None else part + add
            lane += piece.shape[0]
        sums_ref[:, d : d + CHUNK] = part.astype(jnp.bfloat16)
    ones = jnp.ones((weight.shape[1], BLK), jnp.bfloat16)
    total = jnp.dot(weight[...], ones, preferred_element_type=jnp.float32)
    sums_ref[:, width:] = two_pieces(total)


def two_pieces(total):
    high = total.astype(jnp.bfloat16).astype(jnp.float32)
    lane = lax.broadcasted_iota(jnp.int32, total.shape, 1)
    return jnp.where(lane == 0, high, total - high).astype(jnp.bfloat16)


def add_up(sums_ref):
    sums = sums_ref[0].astype(jnp.float32)
    for k in range(1, sums_ref.shape[0]):
        sums = sums + sums_ref[k].astype(jnp.float32)
    return sums


def divide_kernel(sums_ref, out_ref):
    width = out_ref.shape[1]
    sums = add_up(sums_ref)
    total = sums[:, width : width + 1] + sums[:, width + 1 : width + 2]
    out_ref[...] = (sums[:, :width] / total).astype(out_ref.dtype)


def call(kernel, shapes, scratch, args, limit, specs=None):
    vmem = pl.BlockSpec(memory_space=pltpu.VMEM)
    return pl.pallas_call(
        kernel,
        out_shape=shapes,
        in_specs=specs or [vmem] * len(args),
        out_specs=jax.tree.map(lambda _: vmem, shapes),
        scratch_shapes=scratch,
        compiler_params=pltpu.CompilerParams(vmem_limit_bytes=limit * MIB),
    )(*args)


def shape(*dims, dtype=jnp.float32):
    return jax.ShapeDtypeStruct(dims, dtype)


def spread(x, axis):
    return lax.all_to_all(x, axis, 0, 0, tiled=True)


def move(x, place):
    pairs = []
    for z in range(CHIPS):
        for c in range(CORES):
            to = place(z, c)
            pairs.append((z * CORES + c, to[0] % CHIPS * CORES + to[1]))
    return lax.ppermute(x, "row", pairs)


def ring(x):
    return move(x, lambda z, c: (z + 1 - 2 * c, c))


def partner(x):
    return move(x, lambda z, c: (z, 1 - c))


def held_order():
    row = lax.axis_index("row")
    z, c = row // CORES, row % CORES
    way = 2 * c - 1
    order = []
    for k in (0, 1, 2, 3, -1, -2, -3, 4):
        chip = (z + way * k + CHIPS) % CHIPS
        core = c if k >= 0 else 1 - c
        order += [chip * CORES + core, chip * CORES + 1 - core]
    return order


def held_slots():
    row = lax.axis_index("row")
    z, c = row // CORES, row % CORES
    way = 2 * c - 1
    slots = []
    for cluster in range(CHIPS * CORES):
        k = ((cluster // CORES - z) * way + CHIPS) % CHIPS
        second = jnp.where(cluster % CORES == c, 0, 1)
        mirrored = jnp.where(k == 4, 14 + second, 8 + 2 * (7 - k) + 1 - second)
        slots.append(jnp.where(k < 4, 2 * k + second, mirrored))
    return slots


def body(source, target, source_mass, target_mass, tile_src, tile_dst, tile_count):
    rows, cols = lax.axis_size("row"), lax.axis_size("col")
    width = source.shape[1]
    nsrc, ntgt = source_mass.shape[0] // BLK, target_mass.shape[0] // BLK
    near = partner(target)
    one, near_one = ring(target), ring(near)
    src = spread(jnp.broadcast_to(source[None], (cols, *source.shape)), "col")
    src = src.reshape(-1, width)
    two, near_two = ring(one), ring(near_one)
    amass = source_mass.reshape(nsrc, BLK)
    bmass = target_mass.reshape(ntgt, BLK)
    vmem, smem = (pl.BlockSpec(memory_space=space) for space in (pltpu.VMEM, pltpu.SMEM))
    norm, far = call(
        prepare_kernel,
        (shape(src.shape[0], BLK), shape(nsrc * ntgt, BLK)),
        [pltpu.SMEM((ntgt,), jnp.int32)],
        (tile_src.reshape(-1), tile_dst.reshape(-1), tile_count.reshape(-1), src),
        8,
        [smem, smem, smem, vmem],
    )

    three, near_three = ring(two), ring(near_two)
    three, near_three, norm = lax.optimization_barrier((three, near_three, norm))
    last = ring(three)
    own = jnp.concatenate([target, near])
    joined = jnp.concatenate([one, near_one, two, near_two, three, near_three])
    other = partner(joined)
    def costs(first, some, held=(), outs=()):
        return call(
            lambda *refs: cost_kernel(first, len(some), len(held), *refs),
            (shape(src.shape[0], sum(piece.shape[0] for piece in some)), *outs),
            [],
            (src, norm, far, *some, *held),
            12,
        )

    (cost_a,) = costs(0, (own, joined))
    last, cost_a = lax.optimization_barrier((last, cost_a))
    last_other = partner(last)
    (cost_b,) = costs(8, (other,))
    cost_c, part = costs(14, (last, last_other), (cost_a, cost_b), (shape(cols, nsrc, BLK),))
    cost = (cost_a, cost_b, cost_c)
    pieces = (own, joined, other, last, last_other)

    for step in range(ITERS):
        fpot, part = call(
            target_kernel,
            (shape(nsrc, BLK), shape(rows, ntgt, BLK)),
            [pltpu.VMEM((src.shape[0], BLK), jnp.float32)] + [pltpu.VMEM((ntgt, BLK), jnp.float32)] * 2,
            (spread(part, "col"), amass, *cost),
            12,
        )
        parts = spread(part, "row")
        if step < ITERS - 1:
            part = call(
                source_kernel,
                shape(cols, nsrc, BLK),
                [pltpu.VMEM((ntgt, BLK), jnp.float32)],
                (parts, bmass, *cost),
                12,
            )
    gpot, sums = call(
        lambda *refs: map_kernel(len(pieces), *refs),
        (shape(ntgt, BLK), shape(src.shape[0], width + BLK, dtype=jnp.bfloat16)),
        [pltpu.VMEM((src.shape[0], ntgt * BLK), jnp.bfloat16)],
        (parts, bmass, fpot, *pieces, *cost),
        32,
    )
    share = src.shape[0] // cols
    sums = spread(sums.reshape(cols, share, -1), "col")
    mapped = call(divide_kernel, shape(share, width, dtype=jnp.bfloat16), [], (sums,), 8)
    return (fpot.reshape(-1) * UNIT, gpot.reshape(-1) * UNIT, mapped)


def solution(mesh):
    in_specs = (
        P(("row", "col"), None),
        P(("col", "row"), None),
        P("row"),
        P("col"),
        P("row", "col", None),
        P("row", "col", None),
        P("row", "col"),
    )
    out_specs = (P("row"), P("col"), P(("row", "col"), None))
    return jax.shard_map(body, mesh=mesh, in_specs=in_specs, out_specs=out_specs, check_vma=False)
```

```python
import math

import jax
import jax.numpy as jnp
from jax import lax
from jax.experimental import pallas as pl
from jax.experimental.pallas import tpu as pltpu
from jax.sharding import PartitionSpec as P

BLK = 128
ITERS = 3
EPS = 0.02
UNIT = EPS * math.log(2.0)
FAR = 1e30
MIB = 1 << 20
CHIPS, CORES = 8, 2
CHUNK = 256


def nt_dot(a, b):
    return lax.dot_general(a, b, (((1,), (1,)), ((), ())), preferred_element_type=jnp.float32)


def square_sums(rows):
    rows = rows.astype(jnp.float32)
    rows = rows * rows
    total = rows[:, :BLK]
    for d in range(BLK, rows.shape[1], BLK):
        total = total + rows[:, d : d + BLK]
    return total


def lanes_of(row):
    return jnp.transpose(jnp.broadcast_to(row, (BLK, BLK)))


def finish_rows(peak, total):
    peak, total = jnp.transpose(peak), jnp.transpose(total)
    top = jnp.max(peak, axis=0, keepdims=True)
    return top + jnp.log2(jnp.sum(total * jnp.exp2(peak - top), axis=0, keepdims=True))


def tiles_of(cost_refs):
    return [(ref, slice(d, d + BLK)) for ref in cost_refs for d in range(0, ref.shape[1], BLK)]


def source_parts(cost_refs, rows, part_ref):
    tiles = tiles_of(cost_refs)
    for s in range(cost_refs[0].shape[0] // BLK):
        at = slice(s * BLK, (s + 1) * BLK)

        def gap(n):
            ref, lanes = tiles[n]
            return -ref[at, lanes] if rows is None else rows[n] - ref[at, lanes]

        peak = gap(0)
        for n in range(1, len(tiles)):
            peak = jnp.maximum(peak, gap(n))
        total = jnp.exp2(gap(0) - peak)
        for n in range(1, len(tiles)):
            total = total + jnp.exp2(gap(n) - peak)
        row = finish_rows(peak, total)
        for k in range(part_ref.shape[0]):
            part_ref[k, s : s + 1, :] = row


def prepare_kernel(sidx, tidx, live, src_ref, norm_ref, far_ref, slot):
    nsrc = src_ref.shape[0] // BLK
    ntgt = far_ref.shape[0] // nsrc
    scale = 1.0 / (src_ref.shape[1] * UNIT)
    for n, cluster in enumerate(held_order()):
        slot[cluster] = n
    far_ref[...] = jnp.full_like(far_ref, FAR)

    def mark(k, c):
        far_ref[pl.ds(sidx[k] * ntgt + slot[tidx[k]], 1), :] = jnp.zeros((1, BLK), jnp.float32)
        return c

    lax.fori_loop(0, live[0], mark, 0)
    for s in range(nsrc):
        at = slice(s * BLK, (s + 1) * BLK)
        norm = jnp.sum(square_sums(src_ref[at, :]), axis=1, keepdims=True) * scale
        norm_ref[at, :] = jnp.broadcast_to(norm, (BLK, BLK))


def cost_kernel(first, npiece, nheld, src_ref, norm_ref, far_ref, *refs):
    pieces, held, (cost_ref, *more) = refs[:npiece], refs[npiece : npiece + nheld], refs[npiece + nheld :]
    nsrc = src_ref.shape[0] // BLK
    ntgt = far_ref.shape[0] // nsrc
    scale = 1.0 / (src_ref.shape[1] * UNIT)
    lane = 0
    for piece in pieces:
        for row in range(0, piece.shape[0], CHUNK):
            block = piece[row : row + CHUNK, :]
            cross = nt_dot(src_ref[...], block) * (-2.0 * scale)
            for d in range(0, block.shape[0], BLK):
                sums = jnp.transpose(square_sums(block[d : d + BLK, :]))
                norm = jnp.sum(sums, axis=0, keepdims=True) * scale
                for s in range(nsrc):
                    at = slice(s * BLK, (s + 1) * BLK)
                    n = s * ntgt + first + lane // BLK
                    away = norm + far_ref[n : n + 1, :]
                    tile = cross[at, d : d + BLK] + norm_ref[at, :] + away
                    cost_ref[at, lane : lane + BLK] = tile
                lane += BLK
    if more:
        source_parts([*held, cost_ref], None, more[0])


def combine(mass_ref, parts_ref):
    parts = parts_ref[...]
    top = jnp.max(parts, axis=0)
    low = jnp.log2(jnp.sum(jnp.exp2(parts - top[None]), axis=0))
    return jnp.log2(mass_ref[...]) - (top + low)


def target_kernel(parts_ref, mass_ref, *refs):
    *cost_refs, pot_ref, part_ref, wide, held, mine = refs
    pot = combine(mass_ref, parts_ref)
    pot_ref[...] = pot
    for s in range(pot.shape[0]):
        wide[s * BLK : (s + 1) * BLK, :] = lanes_of(pot[s : s + 1, :])
    for n, (ref, lanes) in enumerate(tiles_of(cost_refs)):
        gap = (wide[...] - ref[:, lanes]).reshape(-1, 8, BLK)
        peak = jnp.max(gap, axis=0)
        top = jnp.max(peak, axis=0, keepdims=True)
        total = jnp.sum(jnp.exp2(gap - top[None]), axis=0)
        held[n : n + 1, :] = top + jnp.log2(jnp.sum(total, axis=0, keepdims=True))
    for cluster, slot in enumerate(held_slots()):
        mine[cluster : cluster + 1, :] = held[pl.ds(slot, 1), :]
    part_ref[...] = jnp.broadcast_to(mine[...][None], part_ref.shape)


def held_rows(pot_ref):
    return [pot_ref[pl.ds(cluster, 1), :] for cluster in held_order()]


def source_kernel(parts_ref, mass_ref, *refs):
    *cost_refs, part_ref, pot_ref = refs
    pot_ref[...] = combine(mass_ref, parts_ref)
    source_parts(cost_refs, held_rows(pot_ref), part_ref)


def map_kernel(npiece, parts_ref, mass_ref, fpot_ref, *refs):
    pieces, (*cost_refs, pot_ref, sums_ref, weight) = refs[:npiece], refs[npiece:]
    pot_ref[...] = combine(mass_ref, parts_ref)
    rows = held_rows(pot_ref)
    width = pieces[0].shape[1]
    for s in range(fpot_ref.shape[0]):
        at = slice(s * BLK, (s + 1) * BLK)
        mine = lanes_of(fpot_ref[s : s + 1, :])
        for n, (ref, lanes) in enumerate(tiles_of(cost_refs)):
            power = jnp.exp2(mine + rows[n] - ref[at, lanes])
            weight[at, n * BLK : (n + 1) * BLK] = power.astype(jnp.bfloat16)
    for d in range(0, width, CHUNK):
        part, lane = None, 0
        for piece in pieces:
            low = weight[:, lane : lane + piece.shape[0]]
            add = jnp.dot(low, piece[:, d : d + CHUNK], preferred_element_type=jnp.float32)
            part = add if part is None else part + add
            lane += piece.shape[0]
        sums_ref[:, d : d + CHUNK] = part.astype(jnp.bfloat16)
    ones = jnp.ones((weight.shape[1], BLK), jnp.bfloat16)
    total = jnp.dot(weight[...], ones, preferred_element_type=jnp.float32)
    sums_ref[:, width:] = two_pieces(total)


def two_pieces(total):
    high = total.astype(jnp.bfloat16).astype(jnp.float32)
    lane = lax.broadcasted_iota(jnp.int32, total.shape, 1)
    return jnp.where(lane == 0, high, total - high).astype(jnp.bfloat16)


def add_up(sums_ref):
    sums = sums_ref[0].astype(jnp.float32)
    for k in range(1, sums_ref.shape[0]):
        sums = sums + sums_ref[k].astype(jnp.float32)
    return sums


def divide_kernel(sums_ref, out_ref):
    width = out_ref.shape[1]
    sums = add_up(sums_ref)
    total = sums[:, width : width + 1] + sums[:, width + 1 : width + 2]
    out_ref[...] = (sums[:, :width] / total).astype(out_ref.dtype)


def call(kernel, shapes, scratch, args, limit, specs=None):
    vmem = pl.BlockSpec(memory_space=pltpu.VMEM)
    return pl.pallas_call(
        kernel,
        out_shape=shapes,
        in_specs=specs or [vmem] * len(args),
        out_specs=jax.tree.map(lambda _: vmem, shapes),
        scratch_shapes=scratch,
        compiler_params=pltpu.CompilerParams(vmem_limit_bytes=limit * MIB),
    )(*args)


def shape(*dims, dtype=jnp.float32):
    return jax.ShapeDtypeStruct(dims, dtype)


def spread(x, axis):
    return lax.all_to_all(x, axis, 0, 0, tiled=True)


def move(x, place):
    pairs = []
    for z in range(CHIPS):
        for c in range(CORES):
            to = place(z, c)
            pairs.append((z * CORES + c, to[0] % CHIPS * CORES + to[1]))
    return lax.ppermute(x, "row", pairs)


def ring(x):
    return move(x, lambda z, c: (z + 1 - 2 * c, c))


def partner(x):
    return move(x, lambda z, c: (z, 1 - c))


def held_order():
    row = lax.axis_index("row")
    z, c = row // CORES, row % CORES
    way = 2 * c - 1
    order = []
    for k in (0, 1, 2, 3, -1, -2, -3, 4):
        chip = (z + way * k + CHIPS) % CHIPS
        core = c if k >= 0 else 1 - c
        order += [chip * CORES + core, chip * CORES + 1 - core]
    return order


def held_slots():
    row = lax.axis_index("row")
    z, c = row // CORES, row % CORES
    way = 2 * c - 1
    slots = []
    for cluster in range(CHIPS * CORES):
        k = ((cluster // CORES - z) * way + CHIPS) % CHIPS
        second = jnp.where(cluster % CORES == c, 0, 1)
        mirrored = jnp.where(k == 4, 14 + second, 8 + 2 * (7 - k) + 1 - second)
        slots.append(jnp.where(k < 4, 2 * k + second, mirrored))
    return slots


def body(source, target, source_mass, target_mass, tile_src, tile_dst, tile_count):
    rows, cols = lax.axis_size("row"), lax.axis_size("col")
    width = source.shape[1]
    nsrc, ntgt = source_mass.shape[0] // BLK, target_mass.shape[0] // BLK
    near = partner(target)
    one, near_one = ring(target), ring(near)
    src = spread(jnp.broadcast_to(source[None], (cols, *source.shape)), "col")
    src = src.reshape(-1, width)
    two, near_two = ring(one), ring(near_one)
    amass = source_mass.reshape(nsrc, BLK)
    bmass = target_mass.reshape(ntgt, BLK)
    vmem, smem = (pl.BlockSpec(memory_space=space) for space in (pltpu.VMEM, pltpu.SMEM))
    norm, far = call(
        prepare_kernel,
        (shape(src.shape[0], BLK), shape(nsrc * ntgt, BLK)),
        [pltpu.SMEM((ntgt,), jnp.int32)],
        (tile_src.reshape(-1), tile_dst.reshape(-1), tile_count.reshape(-1), src),
        8,
        [smem, smem, smem, vmem],
    )

    three, near_three = ring(two), ring(near_two)
    three, norm = lax.optimization_barrier((three, norm))
    last = ring(three)
    own = jnp.concatenate([target, near])
    joined = jnp.concatenate([one, near_one, two, near_two, three, near_three])
    last, turn = lax.optimization_barrier((last, joined))
    other = partner(turn)

    def costs(first, some, held=(), outs=()):
        return call(
            lambda *refs: cost_kernel(first, len(some), len(held), *refs),
            (shape(src.shape[0], sum(piece.shape[0] for piece in some)), *outs),
            [],
            (src, norm, far, *some, *held),
            12,
        )

    (cost_a,) = costs(0, (own, joined))
    last, cost_a = lax.optimization_barrier((last, cost_a))
    last_other = partner(last)
    (cost_c,) = costs(14, (last, last_other))
    cost_b, part = costs(8, (other,), (cost_a, cost_c), (shape(cols, nsrc, BLK),))
    cost = (cost_a, cost_b, cost_c)
    pieces = (own, joined, other, last, last_other)

    for step in range(ITERS):
        fpot, part = call(
            target_kernel,
            (shape(nsrc, BLK), shape(rows, ntgt, BLK)),
            [pltpu.VMEM((src.shape[0], BLK), jnp.float32)] + [pltpu.VMEM((ntgt, BLK), jnp.float32)] * 2,
            (spread(part, "col"), amass, *cost),
            12,
        )
        parts = spread(part, "row")
        if step < ITERS - 1:
            part = call(
                source_kernel,
                shape(cols, nsrc, BLK),
                [pltpu.VMEM((ntgt, BLK), jnp.float32)],
                (parts, bmass, *cost),
                12,
            )
    gpot, sums = call(
        lambda *refs: map_kernel(len(pieces), *refs),
        (shape(ntgt, BLK), shape(src.shape[0], width + BLK, dtype=jnp.bfloat16)),
        [pltpu.VMEM((src.shape[0], ntgt * BLK), jnp.bfloat16)],
        (parts, bmass, fpot, *pieces, *cost),
        32,
    )
    share = src.shape[0] // cols
    sums = spread(sums.reshape(cols, share, -1), "col")
    mapped = call(divide_kernel, shape(share, width, dtype=jnp.bfloat16), [], (sums,), 8)
    return (fpot.reshape(-1) * UNIT, gpot.reshape(-1) * UNIT, mapped)


def solution(mesh):
    in_specs = (
        P(("row", "col"), None),
        P(("col", "row"), None),
        P("row"),
        P("col"),
        P("row", "col", None),
        P("row", "col", None),
        P("row", "col"),
    )
    out_specs = (P("row"), P("col"), P(("row", "col"), None))
    return jax.shard_map(body, mesh=mesh, in_specs=in_specs, out_specs=out_specs, check_vma=False)
```

```python
import math

import jax
import jax.numpy as jnp
from jax import lax
from jax.experimental import pallas as pl
from jax.experimental.pallas import tpu as pltpu
from jax.sharding import PartitionSpec as P

BLK = 128
ITERS = 3
EPS = 0.02
UNIT = EPS * math.log(2.0)
FAR = 1e30
MIB = 1 << 20
CHIPS, CORES = 8, 2
CHUNK = 256
COSTS = 3
TOTALS = 8


def nt_dot(a, b):
    return lax.dot_general(a, b, (((1,), (1,)), ((), ())), preferred_element_type=jnp.float32)


def square_sums(rows):
    rows = rows.astype(jnp.float32)
    rows = rows * rows
    total = rows[:, :BLK]
    for d in range(BLK, rows.shape[1], BLK):
        total = total + rows[:, d : d + BLK]
    return total


def lanes_of(row):
    return jnp.transpose(jnp.broadcast_to(row, (BLK, BLK)))


def finish_rows(peak, total):
    peak, total = jnp.transpose(peak), jnp.transpose(total)
    top = jnp.max(peak, axis=0, keepdims=True)
    return top + jnp.log2(jnp.sum(total * jnp.exp2(peak - top), axis=0, keepdims=True))


def tiles_of(cost_refs):
    return [(ref, slice(d, d + BLK)) for ref in cost_refs for d in range(0, ref.shape[1], BLK)]


def source_parts(cost_refs, rows, part_ref):
    tiles = tiles_of(cost_refs)
    for s in range(cost_refs[0].shape[0] // BLK):
        at = slice(s * BLK, (s + 1) * BLK)

        def gap(n):
            ref, lanes = tiles[n]
            return -ref[at, lanes] if rows is None else rows[n] - ref[at, lanes]

        peak = gap(0)
        for n in range(1, len(tiles)):
            peak = jnp.maximum(peak, gap(n))
        total = jnp.exp2(gap(0) - peak)
        for n in range(1, len(tiles)):
            total = total + jnp.exp2(gap(n) - peak)
        row = finish_rows(peak, total)
        for k in range(part_ref.shape[0]):
            part_ref[k, s : s + 1, :] = row


def prepare_kernel(sidx, tidx, live, src_ref, norm_ref, far_ref, slot):
    nsrc = src_ref.shape[0] // BLK
    ntgt = far_ref.shape[0] // nsrc
    scale = 1.0 / (src_ref.shape[1] * UNIT)
    for n, cluster in enumerate(held_order()):
        slot[cluster] = n
    far_ref[...] = jnp.full_like(far_ref, FAR)

    def mark(k, c):
        far_ref[pl.ds(sidx[k] * ntgt + slot[tidx[k]], 1), :] = jnp.zeros((1, BLK), jnp.float32)
        return c

    lax.fori_loop(0, live[0], mark, 0)
    for s in range(nsrc):
        at = slice(s * BLK, (s + 1) * BLK)
        norm = jnp.sum(square_sums(src_ref[at, :]), axis=1, keepdims=True) * scale
        norm_ref[at, :] = jnp.broadcast_to(norm, (BLK, BLK))


def cost_kernel(first, npiece, nheld, src_ref, norm_ref, far_ref, *refs):
    pieces, held, (cost_ref, *more) = refs[:npiece], refs[npiece : npiece + nheld], refs[npiece + nheld :]
    nsrc = src_ref.shape[0] // BLK
    ntgt = far_ref.shape[0] // nsrc
    scale = 1.0 / (src_ref.shape[1] * UNIT)
    lane = 0
    for piece in pieces:
        for row in range(0, piece.shape[0], CHUNK):
            block = piece[row : row + CHUNK, :]
            cross = nt_dot(src_ref[...], block) * (-2.0 * scale)
            for d in range(0, block.shape[0], BLK):
                sums = jnp.transpose(square_sums(block[d : d + BLK, :]))
                norm = jnp.sum(sums, axis=0, keepdims=True) * scale
                for s in range(nsrc):
                    at = slice(s * BLK, (s + 1) * BLK)
                    n = s * ntgt + first + lane // BLK
                    away = norm + far_ref[n : n + 1, :]
                    tile = cross[at, d : d + BLK] + norm_ref[at, :] + away
                    cost_ref[at, lane : lane + BLK] = tile
                lane += BLK
    if more:
        source_parts([*held, cost_ref], None, more[0])


def combine(mass_ref, parts_ref):
    parts = parts_ref[...]
    top = jnp.max(parts, axis=0)
    low = jnp.log2(jnp.sum(jnp.exp2(parts - top[None]), axis=0))
    return jnp.log2(mass_ref[...]) - (top + low)


def target_kernel(parts_ref, mass_ref, *refs):
    *refs, part_ref, wide, held, mine = refs
    cost_refs, pot_refs = refs[:COSTS], refs[COSTS:]
    pot = combine(mass_ref, parts_ref)
    for pot_ref in pot_refs:
        pot_ref[...] = pot
    for s in range(pot.shape[0]):
        wide[s * BLK : (s + 1) * BLK, :] = lanes_of(pot[s : s + 1, :])
    for n, (ref, lanes) in enumerate(tiles_of(cost_refs)):
        gap = (wide[...] - ref[:, lanes]).reshape(-1, 8, BLK)
        peak = jnp.max(gap, axis=0)
        top = jnp.max(peak, axis=0, keepdims=True)
        total = jnp.sum(jnp.exp2(gap - top[None]), axis=0)
        held[n : n + 1, :] = top + jnp.log2(jnp.sum(total, axis=0, keepdims=True))
    for cluster, slot in enumerate(held_slots()):
        mine[cluster : cluster + 1, :] = held[pl.ds(slot, 1), :]
    part_ref[...] = jnp.broadcast_to(mine[...][None], part_ref.shape)


def held_rows(pot_ref):
    return [pot_ref[pl.ds(cluster, 1), :] for cluster in held_order()]


def source_kernel(parts_ref, mass_ref, *refs):
    *cost_refs, part_ref, pot_ref = refs
    pot_ref[...] = combine(mass_ref, parts_ref)
    source_parts(cost_refs, held_rows(pot_ref), part_ref)


def map_kernel(npiece, parts_ref, mass_ref, fpot_ref, *refs):
    pieces, (*cost_refs, fout_ref, gout_ref, sums, pot_ref, weight) = refs[:npiece], refs[npiece:]
    pot = combine(mass_ref, parts_ref)
    pot_ref[...] = pot
    gout_ref[...] = pot * UNIT
    fout_ref[...] = fpot_ref[...] * UNIT
    rows = held_rows(pot_ref)
    width = pieces[0].shape[1]
    for s in range(fpot_ref.shape[0]):
        at = slice(s * BLK, (s + 1) * BLK)
        mine = lanes_of(fpot_ref[s : s + 1, :])
        for n, (ref, lanes) in enumerate(tiles_of(cost_refs)):
            power = jnp.exp2(mine + rows[n] - ref[at, lanes])
            weight[at, n * BLK : (n + 1) * BLK] = power.astype(jnp.bfloat16)
    peers = sums.shape[0]
    share = weight.shape[0] // peers

    ones = jnp.ones((weight.shape[1], BLK), jnp.bfloat16)
    total = jnp.dot(weight[...], ones, preferred_element_type=jnp.float32)
    top = share * width // BLK
    for s in range(fpot_ref.shape[0]):
        tile = jnp.transpose(total[s * BLK : (s + 1) * BLK, :])[:TOTALS, :]
        high = tile.astype(jnp.bfloat16).astype(jnp.float32)
        row = lax.broadcasted_iota(jnp.int32, tile.shape, 0)
        tile = jnp.where(row == 0, high, jnp.where(row == 1, tile - high, 0.0)).astype(jnp.bfloat16)
        for k in range(s * BLK // share, (s + 1) * BLK // share):
            sums[k, top : top + TOTALS, :] = tile
    for d in range(0, width, CHUNK):
        part, lane = None, 0
        for piece in pieces:
            low = weight[:, lane : lane + piece.shape[0]]
            add = jnp.dot(low, piece[:, d : d + CHUNK], preferred_element_type=jnp.float32)
            part = add if part is None else part + add
            lane += piece.shape[0]
        part = part.astype(jnp.bfloat16)
        top = share * d // BLK
        for e in range(0, CHUNK, BLK):
            at = slice(top + share * e // BLK, top + share * (e // BLK + 1))
            for k in range(peers):
                sums[k, at, :] = part[k * share : (k + 1) * share, e : e + BLK]


def divide_kernel(sums_ref, out_ref, totals):
    sums = sums_ref[0].astype(jnp.float32)
    for k in range(1, sums_ref.shape[0]):
        sums = sums + sums_ref[k].astype(jnp.float32)
    share, width = out_ref.shape
    top = share * width // BLK
    totals[...] = lanes_of(sums[top : top + 1, :] + sums[top + 1 : top + 2, :])
    first = lax.axis_index("col") % (BLK // share) * share
    total = totals[pl.ds(pl.multiple_of(first, share), share), :]
    for d in range(width // BLK):
        block = sums[d * share : (d + 1) * share, :] / total
        out_ref[:, d * BLK : (d + 1) * BLK] = block.astype(out_ref.dtype)


def call(kernel, shapes, scratch, args, limit, specs=None):
    vmem = pl.BlockSpec(memory_space=pltpu.VMEM)
    return pl.pallas_call(
        kernel,
        out_shape=shapes,
        in_specs=specs or [vmem] * len(args),
        out_specs=jax.tree.map(lambda _: vmem, shapes),
        scratch_shapes=scratch,
        compiler_params=pltpu.CompilerParams(vmem_limit_bytes=limit * MIB),
    )(*args)


def shape(*dims, dtype=jnp.float32):
    return jax.ShapeDtypeStruct(dims, dtype)


def spread(x, axis):
    return lax.all_to_all(x, axis, 0, 0, tiled=True)


def move(x, place):
    pairs = []
    for z in range(CHIPS):
        for c in range(CORES):
            to = place(z, c)
            pairs.append((z * CORES + c, to[0] % CHIPS * CORES + to[1]))
    return lax.ppermute(x, "row", pairs)


def ring(x):
    return move(x, lambda z, c: (z + 1 - 2 * c, c))


def partner(x):
    return move(x, lambda z, c: (z, 1 - c))


def held_order():
    row = lax.axis_index("row")
    z, c = row // CORES, row % CORES
    way = 2 * c - 1
    order = []
    for k in (0, 1, 2, 3, -1, -2, -3, 4):
        chip = (z + way * k + CHIPS) % CHIPS
        core = c if k >= 0 else 1 - c
        order += [chip * CORES + core, chip * CORES + 1 - core]
    return order


def held_slots():
    row = lax.axis_index("row")
    z, c = row // CORES, row % CORES
    way = 2 * c - 1
    slots = []
    for cluster in range(CHIPS * CORES):
        k = ((cluster // CORES - z) * way + CHIPS) % CHIPS
        second = jnp.where(cluster % CORES == c, 0, 1)
        mirrored = jnp.where(k == 4, 14 + second, 8 + 2 * (7 - k) + 1 - second)
        slots.append(jnp.where(k < 4, 2 * k + second, mirrored))
    return slots


def body(source, target, source_mass, target_mass, tile_src, tile_dst, tile_count):
    rows, cols = lax.axis_size("row"), lax.axis_size("col")
    width = source.shape[1]
    nsrc, ntgt = source_mass.shape[0] // BLK, target_mass.shape[0] // BLK
    near = partner(target)
    one, near_one = ring(target), ring(near)
    src = spread(jnp.broadcast_to(source[None], (cols, *source.shape)), "col")
    src = src.reshape(-1, width)
    two, near_two = ring(one), ring(near_one)
    amass = source_mass.reshape(nsrc, BLK)
    bmass = target_mass.reshape(ntgt, BLK)
    vmem, smem = (pl.BlockSpec(memory_space=space) for space in (pltpu.VMEM, pltpu.SMEM))
    norm, far = call(
        prepare_kernel,
        (shape(src.shape[0], BLK), shape(nsrc * ntgt, BLK)),
        [pltpu.SMEM((ntgt,), jnp.int32)],
        (tile_src.reshape(-1), tile_dst.reshape(-1), tile_count.reshape(-1), src),
        8,
        [smem, smem, smem, vmem],
    )

    three, near_three = ring(two), ring(near_two)
    three, norm = lax.optimization_barrier((three, norm))
    last = ring(three)
    own = jnp.concatenate([target, near])
    joined = jnp.concatenate([one, near_one, two, near_two, three, near_three])
    last, turn = lax.optimization_barrier((last, joined))
    other = partner(turn)

    def costs(first, some, held=(), outs=()):
        return call(
            lambda *refs: cost_kernel(first, len(some), len(held), *refs),
            (shape(src.shape[0], sum(piece.shape[0] for piece in some)), *outs),
            [],
            (src, norm, far, *some, *held),
            12,
        )

    (cost_a,) = costs(0, (own, joined))
    last, cost_a = lax.optimization_barrier((last, cost_a))
    last_other = partner(last)
    (cost_c,) = costs(14, (last, last_other))
    cost_b, part = costs(8, (other,), (cost_a, cost_c), (shape(cols, nsrc, BLK),))
    cost = (cost_a, cost_b, cost_c)
    pieces = (own, joined, other, last, last_other)

    for step in range(ITERS):
        last_step = step == ITERS - 1
        *fpot, part = call(
            target_kernel,
            (shape(nsrc, BLK),) * last_step + (shape(rows, ntgt, BLK),),
            [pltpu.VMEM((src.shape[0], BLK), jnp.float32)] + [pltpu.VMEM((ntgt, BLK), jnp.float32)] * 2,
            (spread(part, "col"), amass, *cost),
            12,
        )
        parts = spread(part, "row")
        if not last_step:
            part = call(
                source_kernel,
                shape(cols, nsrc, BLK),
                [pltpu.VMEM((ntgt, BLK), jnp.float32)],
                (parts, bmass, *cost),
                12,
            )
    (fpot,) = fpot
    share = src.shape[0] // cols
    packed = shape(cols, share * width // BLK + TOTALS, BLK, dtype=jnp.bfloat16)
    fout, gout, sums = call(
        lambda *refs: map_kernel(len(pieces), *refs),
        (shape(nsrc, BLK), shape(ntgt, BLK), packed),
        [
            pltpu.VMEM((ntgt, BLK), jnp.float32),
            pltpu.VMEM((src.shape[0], ntgt * BLK), jnp.bfloat16),
        ],
        (parts, bmass, fpot, *pieces, *cost),
        24,
    )
    sums = spread(sums, "col")
    totals = [pltpu.VMEM((BLK, BLK), jnp.float32)]
    mapped = call(divide_kernel, shape(share, width, dtype=jnp.bfloat16), totals, (sums,), 8)
    return (fout.reshape(-1), gout.reshape(-1), mapped)


def solution(mesh):
    in_specs = (
        P(("row", "col"), None),
        P(("col", "row"), None),
        P("row"),
        P("col"),
        P("row", "col", None),
        P("row", "col", None),
        P("row", "col"),
    )
    out_specs = (P("row"), P("col"), P(("row", "col"), None))
    return jax.shard_map(body, mesh=mesh, in_specs=in_specs, out_specs=out_specs, check_vma=False)
```

```python
import math

import jax
import jax.numpy as jnp
from jax import lax
from jax.experimental import pallas as pl
from jax.experimental.pallas import tpu as pltpu
from jax.sharding import PartitionSpec as P

BLK = 128
ITERS = 3
EPS = 0.02
UNIT = EPS * math.log(2.0)
FAR = 1e30
MIB = 1 << 20
CHIPS, CORES = 8, 2
CHUNK = 256
COSTS = 3
TOTALS = 8


def nt_dot(a, b):
    return lax.dot_general(a, b, (((1,), (1,)), ((), ())), preferred_element_type=jnp.float32)


def square_sums(rows):
    rows = rows.astype(jnp.float32)
    rows = rows * rows
    total = rows[:, :BLK]
    for d in range(BLK, rows.shape[1], BLK):
        total = total + rows[:, d : d + BLK]
    return total


def lanes_of(row):
    return jnp.transpose(jnp.broadcast_to(row, (BLK, BLK)))


def finish_rows(peak, total):
    peak, total = jnp.transpose(peak), jnp.transpose(total)
    top = jnp.max(peak, axis=0, keepdims=True)
    return top + jnp.log2(jnp.sum(total * jnp.exp2(peak - top), axis=0, keepdims=True))


def tiles_of(cost_refs):
    return [(ref, slice(d, d + BLK)) for ref in cost_refs for d in range(0, ref.shape[1], BLK)]


def source_parts(cost_refs, rows, part_ref):
    tiles = tiles_of(cost_refs)
    for s in range(cost_refs[0].shape[0] // BLK):
        at = slice(s * BLK, (s + 1) * BLK)

        def gap(n):
            ref, lanes = tiles[n]
            return -ref[at, lanes] if rows is None else rows[n] - ref[at, lanes]

        peak = gap(0)
        for n in range(1, len(tiles)):
            peak = jnp.maximum(peak, gap(n))
        total = jnp.exp2(gap(0) - peak)
        for n in range(1, len(tiles)):
            total = total + jnp.exp2(gap(n) - peak)
        row = finish_rows(peak, total)
        for k in range(part_ref.shape[0]):
            part_ref[k, s : s + 1, :] = row


def prepare_kernel(sidx, tidx, live, src_ref, norm_ref, far_ref, slot):
    nsrc = src_ref.shape[0] // BLK
    ntgt = far_ref.shape[0] // nsrc
    scale = 1.0 / (src_ref.shape[1] * UNIT)
    for n, cluster in enumerate(held_order()):
        slot[cluster] = n
    far_ref[...] = jnp.full_like(far_ref, FAR)

    def mark(k, c):
        far_ref[pl.ds(sidx[k] * ntgt + slot[tidx[k]], 1), :] = jnp.zeros((1, BLK), jnp.float32)
        return c

    lax.fori_loop(0, live[0], mark, 0)
    for s in range(nsrc):
        at = slice(s * BLK, (s + 1) * BLK)
        norm = jnp.sum(square_sums(src_ref[at, :]), axis=1, keepdims=True) * scale
        norm_ref[at, :] = jnp.broadcast_to(norm, (BLK, BLK))


def cost_kernel(first, npiece, nheld, src_ref, norm_ref, far_ref, *refs):
    pieces, held, (cost_ref, *more) = refs[:npiece], refs[npiece : npiece + nheld], refs[npiece + nheld :]
    nsrc = src_ref.shape[0] // BLK
    ntgt = far_ref.shape[0] // nsrc
    scale = 1.0 / (src_ref.shape[1] * UNIT)
    lane = 0
    for piece in pieces:
        for row in range(0, piece.shape[0], CHUNK):
            block = piece[row : row + CHUNK, :]
            cross = nt_dot(src_ref[...], block) * (-2.0 * scale)
            for d in range(0, block.shape[0], BLK):
                sums = jnp.transpose(square_sums(block[d : d + BLK, :]))
                norm = jnp.sum(sums, axis=0, keepdims=True) * scale
                for s in range(nsrc):
                    at = slice(s * BLK, (s + 1) * BLK)
                    n = s * ntgt + first + lane // BLK
                    away = norm + far_ref[n : n + 1, :]
                    tile = cross[at, d : d + BLK] + norm_ref[at, :] + away
                    cost_ref[at, lane : lane + BLK] = tile
                lane += BLK
    if more:
        source_parts([*held, cost_ref], None, more[0])


def combine(mass_ref, parts_ref):
    parts = parts_ref[...]
    top = jnp.max(parts, axis=0)
    low = jnp.log2(jnp.sum(jnp.exp2(parts - top[None]), axis=0))
    return jnp.log2(mass_ref[...]) - (top + low)


def target_kernel(parts_ref, mass_ref, *refs):
    *refs, part_ref, wide, held, mine = refs
    cost_refs, pot_refs = refs[:COSTS], refs[COSTS:]
    pot = combine(mass_ref, parts_ref)
    for pot_ref in pot_refs:
        pot_ref[...] = pot
    for s in range(pot.shape[0]):
        wide[s * BLK : (s + 1) * BLK, :] = lanes_of(pot[s : s + 1, :])
    for n, (ref, lanes) in enumerate(tiles_of(cost_refs)):
        gap = (wide[...] - ref[:, lanes]).reshape(-1, 8, BLK)
        peak = jnp.max(gap, axis=0)
        top = jnp.max(peak, axis=0, keepdims=True)
        total = jnp.sum(jnp.exp2(gap - top[None]), axis=0)
        held[n : n + 1, :] = top + jnp.log2(jnp.sum(total, axis=0, keepdims=True))
    for cluster, slot in enumerate(held_slots()):
        mine[cluster : cluster + 1, :] = held[pl.ds(slot, 1), :]
    part_ref[...] = jnp.broadcast_to(mine[...][None], part_ref.shape)


def held_rows(pot_ref):
    return [pot_ref[pl.ds(cluster, 1), :] for cluster in held_order()]


def source_kernel(parts_ref, mass_ref, *refs):
    *cost_refs, part_ref, pot_ref = refs
    pot_ref[...] = combine(mass_ref, parts_ref)
    source_parts(cost_refs, held_rows(pot_ref), part_ref)


def map_kernel(npiece, parts_ref, mass_ref, fpot_ref, *refs):
    pieces, (*cost_refs, fout_ref, gout_ref, sums, pot_ref, weight) = refs[:npiece], refs[npiece:]
    pot = combine(mass_ref, parts_ref)
    pot_ref[...] = pot
    gout_ref[...] = pot * UNIT
    fout_ref[...] = fpot_ref[...] * UNIT
    rows = held_rows(pot_ref)
    width = pieces[0].shape[1]
    for s in range(fpot_ref.shape[0]):
        at = slice(s * BLK, (s + 1) * BLK)
        mine = lanes_of(fpot_ref[s : s + 1, :])
        for n, (ref, lanes) in enumerate(tiles_of(cost_refs)):
            power = jnp.exp2(mine + rows[n] - ref[at, lanes])
            weight[at, n * BLK : (n + 1) * BLK] = power.astype(jnp.bfloat16)
    peers = sums.shape[0]
    share = weight.shape[0] // peers

    ones = jnp.ones((weight.shape[1], BLK), jnp.bfloat16)
    total = jnp.dot(weight[...], ones, preferred_element_type=jnp.float32)
    top = share * width // BLK
    for s in range(fpot_ref.shape[0]):
        tile = jnp.transpose(total[s * BLK : (s + 1) * BLK, :])[:TOTALS, :]
        high = tile.astype(jnp.bfloat16).astype(jnp.float32)
        row = lax.broadcasted_iota(jnp.int32, tile.shape, 0)
        tile = jnp.where(row == 0, high, jnp.where(row == 1, tile - high, 0.0)).astype(jnp.bfloat16)
        for k in range(s * BLK // share, (s + 1) * BLK // share):
            sums[k, top : top + TOTALS, :] = tile
    for d in range(0, width, CHUNK):
        part, lane = None, 0
        for piece in pieces:
            low = weight[:, lane : lane + piece.shape[0]]
            add = jnp.dot(low, piece[:, d : d + CHUNK], preferred_element_type=jnp.float32)
            part = add if part is None else part + add
            lane += piece.shape[0]
        part = part.astype(jnp.bfloat16)
        top = share * d // BLK
        for e in range(0, CHUNK, BLK):
            at = slice(top + share * e // BLK, top + share * (e // BLK + 1))
            for k in range(peers):
                sums[k, at, :] = part[k * share : (k + 1) * share, e : e + BLK]


def divide_kernel(sums_ref, out_ref, totals):
    sums = sums_ref[0].astype(jnp.float32)
    for k in range(1, sums_ref.shape[0]):
        sums = sums + sums_ref[k].astype(jnp.float32)
    share, width = out_ref.shape
    top = share * width // BLK
    totals[...] = lanes_of(sums[top : top + 1, :] + sums[top + 1 : top + 2, :])
    first = lax.axis_index("col") % (BLK // share) * share
    total = totals[pl.ds(pl.multiple_of(first, share), share), :]
    for d in range(width // BLK):
        block = sums[d * share : (d + 1) * share, :] / total
        out_ref[:, d * BLK : (d + 1) * BLK] = block.astype(out_ref.dtype)


def call(kernel, shapes, scratch, args, limit, specs=None):
    vmem = pl.BlockSpec(memory_space=pltpu.VMEM)
    return pl.pallas_call(
        kernel,
        out_shape=shapes,
        in_specs=specs or [vmem] * len(args),
        out_specs=jax.tree.map(lambda _: vmem, shapes),
        scratch_shapes=scratch,
        compiler_params=pltpu.CompilerParams(vmem_limit_bytes=limit * MIB),
    )(*args)


def shape(*dims, dtype=jnp.float32):
    return jax.ShapeDtypeStruct(dims, dtype)


def spread(x, axis):
    return lax.all_to_all(x, axis, 0, 0, tiled=True)


def move(x, place):
    pairs = []
    for z in range(CHIPS):
        for c in range(CORES):
            to = place(z, c)
            pairs.append((z * CORES + c, to[0] % CHIPS * CORES + to[1]))
    return lax.ppermute(x, "row", pairs)


def ring(x):
    return move(x, lambda z, c: (z + 1 - 2 * c, c))


def partner(x):
    return move(x, lambda z, c: (z, 1 - c))


def held_order():
    row = lax.axis_index("row")
    z, c = row // CORES, row % CORES
    way = 2 * c - 1
    order = []
    for k in (0, 1, 2, 3, -1, -2, -3, 4):
        chip = (z + way * k + CHIPS) % CHIPS
        core = c if k >= 0 else 1 - c
        order += [chip * CORES + core, chip * CORES + 1 - core]
    return order


def held_slots():
    row = lax.axis_index("row")
    z, c = row // CORES, row % CORES
    way = 2 * c - 1
    slots = []
    for cluster in range(CHIPS * CORES):
        k = ((cluster // CORES - z) * way + CHIPS) % CHIPS
        second = jnp.where(cluster % CORES == c, 0, 1)
        mirrored = jnp.where(k == 4, 14 + second, 8 + 2 * (7 - k) + 1 - second)
        slots.append(jnp.where(k < 4, 2 * k + second, mirrored))
    return slots


def body(source, target, source_mass, target_mass, tile_src, tile_dst, tile_count):
    rows, cols = lax.axis_size("row"), lax.axis_size("col")
    width = source.shape[1]
    nsrc, ntgt = source_mass.shape[0] // BLK, target_mass.shape[0] // BLK
    near = partner(target)
    one, near_one = ring(target), ring(near)
    src = spread(jnp.broadcast_to(source[None], (cols, *source.shape)), "col")
    src = src.reshape(-1, width)
    two, near_two = ring(one), ring(near_one)
    amass = source_mass.reshape(nsrc, BLK)
    bmass = target_mass.reshape(ntgt, BLK)
    vmem, smem = (pl.BlockSpec(memory_space=space) for space in (pltpu.VMEM, pltpu.SMEM))
    norm, far = call(
        prepare_kernel,
        (shape(src.shape[0], BLK), shape(nsrc * ntgt, BLK)),
        [pltpu.SMEM((ntgt,), jnp.int32)],
        (tile_src.reshape(-1), tile_dst.reshape(-1), tile_count.reshape(-1), src),
        8,
        [smem, smem, smem, vmem],
    )

    three, near_three = ring(two), ring(near_two)
    three, norm = lax.optimization_barrier((three, norm))
    last = ring(three)
    own = jnp.concatenate([target, near])
    joined = jnp.concatenate([one, near_one, two, near_two, three, near_three])

    def costs(first, some, held=(), outs=()):
        return call(
            lambda *refs: cost_kernel(first, len(some), len(held), *refs),
            (shape(src.shape[0], sum(piece.shape[0] for piece in some)), *outs),
            [],
            (src, norm, far, *some, *held),
            12,
        )

    (cost_a,) = costs(0, (own, joined))
    last, turn, cost_a = lax.optimization_barrier((last, joined, cost_a))
    other = partner(turn)
    last_other = partner(last)
    (cost_c,) = costs(14, (last, last_other))
    cost_b, part = costs(8, (other,), (cost_a, cost_c), (shape(cols, nsrc, BLK),))
    cost = (cost_a, cost_b, cost_c)
    pieces = (own, joined, other, last, last_other)

    for step in range(ITERS):
        last_step = step == ITERS - 1
        *fpot, part = call(
            target_kernel,
            (shape(nsrc, BLK),) * last_step + (shape(rows, ntgt, BLK),),
            [pltpu.VMEM((src.shape[0], BLK), jnp.float32)] + [pltpu.VMEM((ntgt, BLK), jnp.float32)] * 2,
            (spread(part, "col"), amass, *cost),
            12,
        )
        parts = spread(part, "row")
        if not last_step:
            part = call(
                source_kernel,
                shape(cols, nsrc, BLK),
                [pltpu.VMEM((ntgt, BLK), jnp.float32)],
                (parts, bmass, *cost),
                12,
            )
    (fpot,) = fpot
    share = src.shape[0] // cols
    packed = shape(cols, share * width // BLK + TOTALS, BLK, dtype=jnp.bfloat16)
    fout, gout, sums = call(
        lambda *refs: map_kernel(len(pieces), *refs),
        (shape(nsrc, BLK), shape(ntgt, BLK), packed),
        [
            pltpu.VMEM((ntgt, BLK), jnp.float32),
            pltpu.VMEM((src.shape[0], ntgt * BLK), jnp.bfloat16),
        ],
        (parts, bmass, fpot, *pieces, *cost),
        24,
    )
    sums = spread(sums, "col")
    totals = [pltpu.VMEM((BLK, BLK), jnp.float32)]
    mapped = call(divide_kernel, shape(share, width, dtype=jnp.bfloat16), totals, (sums,), 8)
    return (fout.reshape(-1), gout.reshape(-1), mapped)


def solution(mesh):
    in_specs = (
        P(("row", "col"), None),
        P(("col", "row"), None),
        P("row"),
        P("col"),
        P("row", "col", None),
        P("row", "col", None),
        P("row", "col"),
    )
    out_specs = (P("row"), P("col"), P(("row", "col"), None))
    return jax.shard_map(body, mesh=mesh, in_specs=in_specs, out_specs=out_specs, check_vma=False)
```

```python
import math

import jax
import jax.numpy as jnp
from jax import lax
from jax.experimental import pallas as pl
from jax.experimental.pallas import tpu as pltpu
from jax.sharding import PartitionSpec as P

BLK = 128
ITERS = 3
EPS = 0.02
UNIT = EPS * math.log(2.0)
FAR = 1e30
MIB = 1 << 20
CHIPS, CORES = 8, 2
CHUNK = 256
COSTS = 3
TOTALS = 8


def nt_dot(a, b):
    return lax.dot_general(a, b, (((1,), (1,)), ((), ())), preferred_element_type=jnp.float32)


def square_sums(rows):
    rows = rows.astype(jnp.float32)
    rows = rows * rows
    total = rows[:, :BLK]
    for d in range(BLK, rows.shape[1], BLK):
        total = total + rows[:, d : d + BLK]
    return total


def lanes_of(row):
    return jnp.transpose(jnp.broadcast_to(row, (BLK, BLK)))


def finish_rows(peak, total):
    peak, total = jnp.transpose(peak), jnp.transpose(total)
    top = jnp.max(peak, axis=0, keepdims=True)
    return top + jnp.log2(jnp.sum(total * jnp.exp2(peak - top), axis=0, keepdims=True))


def tiles_of(cost_refs):
    return [(ref, slice(d, d + BLK)) for ref in cost_refs for d in range(0, ref.shape[1], BLK)]


def source_parts(cost_refs, rows, part_ref):
    tiles = tiles_of(cost_refs)
    for s in range(cost_refs[0].shape[0] // BLK):
        at = slice(s * BLK, (s + 1) * BLK)

        def gap(n):
            ref, lanes = tiles[n]
            return -ref[at, lanes] if rows is None else rows[n] - ref[at, lanes]

        peak = gap(0)
        for n in range(1, len(tiles)):
            peak = jnp.maximum(peak, gap(n))
        total = jnp.exp2(gap(0) - peak)
        for n in range(1, len(tiles)):
            total = total + jnp.exp2(gap(n) - peak)
        row = finish_rows(peak, total)
        for k in range(part_ref.shape[0]):
            part_ref[k, s : s + 1, :] = row


def prepare_kernel(sidx, tidx, live, src_ref, norm_ref, far_ref, slot):
    nsrc = src_ref.shape[0] // BLK
    ntgt = far_ref.shape[0] // nsrc
    scale = 1.0 / (src_ref.shape[1] * UNIT)
    for n, cluster in enumerate(held_order()):
        slot[cluster] = n
    far_ref[...] = jnp.full_like(far_ref, FAR)

    def mark(k, c):
        far_ref[pl.ds(sidx[k] * ntgt + slot[tidx[k]], 1), :] = jnp.zeros((1, BLK), jnp.float32)
        return c

    lax.fori_loop(0, live[0], mark, 0)
    for s in range(nsrc):
        at = slice(s * BLK, (s + 1) * BLK)
        norm = jnp.sum(square_sums(src_ref[at, :]), axis=1, keepdims=True) * scale
        norm_ref[at, :] = jnp.broadcast_to(norm, (BLK, BLK))


def cost_kernel(first, npiece, nheld, src_ref, norm_ref, far_ref, *refs):
    pieces, held, (cost_ref, *more) = refs[:npiece], refs[npiece : npiece + nheld], refs[npiece + nheld :]
    nsrc = src_ref.shape[0] // BLK
    ntgt = far_ref.shape[0] // nsrc
    scale = 1.0 / (src_ref.shape[1] * UNIT)
    lane = 0
    for piece in pieces:
        for row in range(0, piece.shape[0], CHUNK):
            block = piece[row : row + CHUNK, :]
            cross = nt_dot(src_ref[...], block) * (-2.0 * scale)
            for d in range(0, block.shape[0], BLK):
                sums = jnp.transpose(square_sums(block[d : d + BLK, :]))
                norm = jnp.sum(sums, axis=0, keepdims=True) * scale
                for s in range(nsrc):
                    at = slice(s * BLK, (s + 1) * BLK)
                    n = s * ntgt + first + lane // BLK
                    away = norm + far_ref[n : n + 1, :]
                    tile = cross[at, d : d + BLK] + norm_ref[at, :] + away
                    cost_ref[at, lane : lane + BLK] = tile
                lane += BLK
    if more:
        source_parts([*held, cost_ref], None, more[0])


def combine(mass_ref, parts_ref):
    parts = parts_ref[...]
    top = jnp.max(parts, axis=0)
    low = jnp.log2(jnp.sum(jnp.exp2(parts - top[None]), axis=0))
    return jnp.log2(mass_ref[...]) - (top + low)


def target_kernel(parts_ref, mass_ref, *refs):
    *refs, part_ref, wide, held, mine = refs
    cost_refs, pot_refs = refs[:COSTS], refs[COSTS:]
    pot = combine(mass_ref, parts_ref)
    for pot_ref in pot_refs:
        pot_ref[...] = pot
    for s in range(pot.shape[0]):
        wide[s * BLK : (s + 1) * BLK, :] = lanes_of(pot[s : s + 1, :])
    for n, (ref, lanes) in enumerate(tiles_of(cost_refs)):
        gap = (wide[...] - ref[:, lanes]).reshape(-1, 8, BLK)
        peak = jnp.max(gap, axis=0)
        top = jnp.max(peak, axis=0, keepdims=True)
        total = jnp.sum(jnp.exp2(gap - top[None]), axis=0)
        held[n : n + 1, :] = top + jnp.log2(jnp.sum(total, axis=0, keepdims=True))
    for cluster, slot in enumerate(held_slots()):
        mine[cluster : cluster + 1, :] = held[pl.ds(slot, 1), :]
    part_ref[...] = jnp.broadcast_to(mine[...][None], part_ref.shape)


def held_rows(pot_ref):
    return [pot_ref[pl.ds(cluster, 1), :] for cluster in held_order()]


def source_kernel(parts_ref, mass_ref, *refs):
    *cost_refs, part_ref, pot_ref = refs
    pot_ref[...] = combine(mass_ref, parts_ref)
    source_parts(cost_refs, held_rows(pot_ref), part_ref)


def map_kernel(npiece, parts_ref, mass_ref, fpot_ref, *refs):
    pieces, (*cost_refs, fout_ref, gout_ref, sums, pot_ref, weight) = refs[:npiece], refs[npiece:]
    pot = combine(mass_ref, parts_ref)
    pot_ref[...] = pot
    gout_ref[...] = pot * UNIT
    fout_ref[...] = fpot_ref[...] * UNIT
    rows = held_rows(pot_ref)
    width = pieces[0].shape[1]
    for s in range(fpot_ref.shape[0]):
        at = slice(s * BLK, (s + 1) * BLK)
        mine = lanes_of(fpot_ref[s : s + 1, :])
        for n, (ref, lanes) in enumerate(tiles_of(cost_refs)):
            power = jnp.exp2(mine + rows[n] - ref[at, lanes])
            weight[at, n * BLK : (n + 1) * BLK] = power.astype(jnp.bfloat16)
    peers = sums.shape[0]
    share = weight.shape[0] // peers

    ones = jnp.ones((weight.shape[1], BLK), jnp.bfloat16)
    total = jnp.dot(weight[...], ones, preferred_element_type=jnp.float32)
    top = share * width // BLK
    for s in range(fpot_ref.shape[0]):
        tile = jnp.transpose(total[s * BLK : (s + 1) * BLK, :])[:TOTALS, :]
        high = tile.astype(jnp.bfloat16).astype(jnp.float32)
        row = lax.broadcasted_iota(jnp.int32, tile.shape, 0)
        tile = jnp.where(row == 0, high, jnp.where(row == 1, tile - high, 0.0)).astype(jnp.bfloat16)
        for k in range(s * BLK // share, (s + 1) * BLK // share):
            sums[k, top : top + TOTALS, :] = tile
    for d in range(0, width, CHUNK):
        part, lane = None, 0
        for piece in pieces:
            low = weight[:, lane : lane + piece.shape[0]]
            add = jnp.dot(low, piece[:, d : d + CHUNK], preferred_element_type=jnp.float32)
            part = add if part is None else part + add
            lane += piece.shape[0]
        part = part.astype(jnp.bfloat16)
        top = share * d // BLK
        for e in range(0, CHUNK, BLK):
            at = slice(top + share * e // BLK, top + share * (e // BLK + 1))
            for k in range(peers):
                sums[k, at, :] = part[k * share : (k + 1) * share, e : e + BLK]


def divide_kernel(sums_ref, out_ref, totals):
    sums = sums_ref[0].astype(jnp.float32)
    for k in range(1, sums_ref.shape[0]):
        sums = sums + sums_ref[k].astype(jnp.float32)
    share, width = out_ref.shape
    top = share * width // BLK
    totals[...] = lanes_of(sums[top : top + 1, :] + sums[top + 1 : top + 2, :])
    first = lax.axis_index("col") % (BLK // share) * share
    total = totals[pl.ds(pl.multiple_of(first, share), share), :]
    for d in range(width // BLK):
        block = sums[d * share : (d + 1) * share, :] / total
        out_ref[:, d * BLK : (d + 1) * BLK] = block.astype(out_ref.dtype)


def call(kernel, shapes, scratch, args, limit, specs=None):
    vmem = pl.BlockSpec(memory_space=pltpu.VMEM)
    return pl.pallas_call(
        kernel,
        out_shape=shapes,
        in_specs=specs or [vmem] * len(args),
        out_specs=jax.tree.map(lambda _: vmem, shapes),
        scratch_shapes=scratch,
        compiler_params=pltpu.CompilerParams(vmem_limit_bytes=limit * MIB),
    )(*args)


def shape(*dims, dtype=jnp.float32):
    return jax.ShapeDtypeStruct(dims, dtype)


def spread(x, axis):
    return lax.all_to_all(x, axis, 0, 0, tiled=True)


def move(x, place):
    pairs = []
    for z in range(CHIPS):
        for c in range(CORES):
            to = place(z, c)
            pairs.append((z * CORES + c, to[0] % CHIPS * CORES + to[1]))
    return lax.ppermute(x, "row", pairs)


def ring(x):
    return move(x, lambda z, c: (z + 1 - 2 * c, c))


def partner(x):
    return move(x, lambda z, c: (z, 1 - c))


def held_order():
    row = lax.axis_index("row")
    z, c = row // CORES, row % CORES
    way = 2 * c - 1
    order = []
    for k in (0, 1, 2, 3, -1, -2, -3, 4):
        chip = (z + way * k + CHIPS) % CHIPS
        core = c if k >= 0 else 1 - c
        order += [chip * CORES + core, chip * CORES + 1 - core]
    return order


def held_slots():
    row = lax.axis_index("row")
    z, c = row // CORES, row % CORES
    way = 2 * c - 1
    slots = []
    for cluster in range(CHIPS * CORES):
        k = ((cluster // CORES - z) * way + CHIPS) % CHIPS
        second = jnp.where(cluster % CORES == c, 0, 1)
        mirrored = jnp.where(k == 4, 14 + second, 8 + 2 * (7 - k) + 1 - second)
        slots.append(jnp.where(k < 4, 2 * k + second, mirrored))
    return slots


def body(source, target, source_mass, target_mass, tile_src, tile_dst, tile_count):
    rows, cols = lax.axis_size("row"), lax.axis_size("col")
    width = source.shape[1]
    nsrc, ntgt = source_mass.shape[0] // BLK, target_mass.shape[0] // BLK
    near = partner(target)
    one, near_one = ring(target), ring(near)
    src = spread(jnp.broadcast_to(source[None], (cols, *source.shape)), "col")
    src = src.reshape(-1, width)
    two, near_two = ring(one), ring(near_one)
    amass = source_mass.reshape(nsrc, BLK)
    bmass = target_mass.reshape(ntgt, BLK)
    vmem, smem = (pl.BlockSpec(memory_space=space) for space in (pltpu.VMEM, pltpu.SMEM))
    norm, far = call(
        prepare_kernel,
        (shape(src.shape[0], BLK), shape(nsrc * ntgt, BLK)),
        [pltpu.SMEM((ntgt,), jnp.int32)],
        (tile_src.reshape(-1), tile_dst.reshape(-1), tile_count.reshape(-1), src),
        8,
        [smem, smem, smem, vmem],
    )

    three, near_three = ring(two), ring(near_two)
    near_three, norm = lax.optimization_barrier((near_three, norm))
    last = ring(three)
    own = jnp.concatenate([target, near])
    joined = jnp.concatenate([one, near_one, two, near_two, three, near_three])

    def costs(first, some, held=(), outs=()):
        return call(
            lambda *refs: cost_kernel(first, len(some), len(held), *refs),
            (shape(src.shape[0], sum(piece.shape[0] for piece in some)), *outs),
            [],
            (src, norm, far, *some, *held),
            12,
        )

    (cost_a,) = costs(0, (own, joined))
    last, turn, cost_a = lax.optimization_barrier((last, joined, cost_a))
    other = partner(turn)
    last_other = partner(last)
    (cost_c,) = costs(14, (last, last_other))
    cost_b, part = costs(8, (other,), (cost_a, cost_c), (shape(cols, nsrc, BLK),))
    cost = (cost_a, cost_b, cost_c)
    pieces = (own, joined, other, last, last_other)

    for step in range(ITERS):
        last_step = step == ITERS - 1
        *fpot, part = call(
            target_kernel,
            (shape(nsrc, BLK),) * last_step + (shape(rows, ntgt, BLK),),
            [pltpu.VMEM((src.shape[0], BLK), jnp.float32)] + [pltpu.VMEM((ntgt, BLK), jnp.float32)] * 2,
            (spread(part, "col"), amass, *cost),
            12,
        )
        parts = spread(part, "row")
        if not last_step:
            part = call(
                source_kernel,
                shape(cols, nsrc, BLK),
                [pltpu.VMEM((ntgt, BLK), jnp.float32)],
                (parts, bmass, *cost),
                12,
            )
    (fpot,) = fpot
    share = src.shape[0] // cols
    packed = shape(cols, share * width // BLK + TOTALS, BLK, dtype=jnp.bfloat16)
    fout, gout, sums = call(
        lambda *refs: map_kernel(len(pieces), *refs),
        (shape(nsrc, BLK), shape(ntgt, BLK), packed),
        [
            pltpu.VMEM((ntgt, BLK), jnp.float32),
            pltpu.VMEM((src.shape[0], ntgt * BLK), jnp.bfloat16),
        ],
        (parts, bmass, fpot, *pieces, *cost),
        24,
    )
    sums = spread(sums, "col")
    totals = [pltpu.VMEM((BLK, BLK), jnp.float32)]
    mapped = call(divide_kernel, shape(share, width, dtype=jnp.bfloat16), totals, (sums,), 8)
    return (fout.reshape(-1), gout.reshape(-1), mapped)


def solution(mesh):
    in_specs = (
        P(("row", "col"), None),
        P(("col", "row"), None),
        P("row"),
        P("col"),
        P("row", "col", None),
        P("row", "col", None),
        P("row", "col"),
    )
    out_specs = (P("row"), P("col"), P(("row", "col"), None))
    return jax.shard_map(body, mesh=mesh, in_specs=in_specs, out_specs=out_specs, check_vma=False)
```
